512 devices in a mesh: seq: 64 (over z, x, core), head: 8 (over y).
Axes of the slice: x: 4, y: 8, z: 8, core: 2. Of those that a mesh axis runs over, the one named last changes fastest.
Arguments:
- queries: float32 [24576, 4096], P('seq', 'head'), may hold values from -1.75 to 1.75
- key_vectors: float32 [24576, 4096], P('seq', 'head'), may hold values from -1.75 to 1.75
- value_vectors: float32 [24576, 4096], P('seq', 'head'), may hold values from -6 to 6
- out_grad: float32 [24576, 4096], P('seq', 'head'), may hold values from -6 to 6
- norm_gain: float32 [4096], P('head'), may hold values from 0.5 to 1.5
- decay_rates: float32 [32], P('head'), may hold values from 4.0690105e-07 to 0.05
- segment_ids: int32 [24576], P('seq'), may hold values from 0 to 5, never falling along the last dimension, each value on 1 to 8192 neighbouring positions
Outputs:
- query_grad: bfloat16 [24576, 4096], P('seq', 'head')
- key_grad: bfloat16 [24576, 4096], P('seq', 'head')
- value_grad: bfloat16 [24576, 4096], P('seq', 'head')
- gain_grad: float32 [4096], P('head')
The draws below stay inside these ranges and needn't reach their ends.
Inputs may be any that keep to these rules, and one draw needn't show every extreme that they name: `segment_ids`: segment numbers never fall along the tokens; each of the 6 segments is one run of 1 to 8192 tokens, and one has exactly 8192.
All inputs are finite; a program needn't handle non-finite values.
Results may differ from the reference program's by a relative error of at most 0.001.
Values sent between devices are 32-bit elements; how exact they have to be, the bound alone decides.
No kernel may reach another device: no remote copies, remote signals or barrier semaphores. Data moves between devices by JAX's collectives and lax.ppermute only.
A program may use at most 128 MiB of HBM per device.

```python
import math
import jax
import jax.numpy as jnp
import numpy as np
from jax import lax

HEAD_DIM = 128
TOK_DEV = 384
SEGS = 6
HEADS = 32
FEAT = 4096
TOKENS = 24576
N_SEQ = 64


def level_of(stream_key, extent, split, smallest, top_value):
    factor_of = 1.0
    for position, parts in split:
        heights = jax.random.uniform(jax.random.fold_in(jax.random.fold_in(stream_key, 6), position), (parts,), jnp.float32, smallest / len(split), top_value / len(split))
        factor_of = factor_of * jnp.repeat(jnp.exp(heights), extent[position] // parts).reshape((-1,) + (1,) * (len(extent) - 1 - position))
    return factor_of


def length_profile(amount, total, most, lean):
    loads = [(1 << 20) // math.isqrt(standing ** lean) + 1 for standing in range(2, amount + 1)]
    surplus, counts = total - most - (amount - 1), [1] * (amount - 1)
    while surplus > 0:
        candidates = [i for i in range(amount - 1) if counts[i] < most]
        whole, budget = sum([loads[i] for i in candidates]), surplus
        for i in candidates:
            addition = min(most - counts[i], max(1, budget * loads[i] // whole), surplus)
            counts[i] = counts[i] + addition
            surplus = surplus - addition
    return np.array([most] + counts)


def ragged(rng, amount, total, bound, skew):
    if amount == 2:
        one = jax.random.randint(rng, (), max(1, total - bound), min(bound, total - 1) + 1)
        return jnp.stack([one, total - one])
    lengths = jnp.asarray(length_profile(amount, total, bound, skew), jnp.int32)
    twos = (amount - 1) // 2
    source_of, taker = lengths[1:1 + 2 * twos:2], lengths[2:2 + 2 * twos:2]
    room = jnp.minimum(source_of - 1, bound - taker)
    moved = jax.random.randint(jax.random.fold_in(rng, 1), (twos,), 0, 1 << 20) % (room + 1)
    lengths = lengths.at[1:1 + 2 * twos:2].set(source_of - moved).at[2:2 + 2 * twos:2].set(taker + moved)
    return lengths[jax.random.permutation(jax.random.fold_in(rng, 2), amount)]


def gaussian(key, shape, width, limit, shards=(), held_as=jnp.bfloat16):
    entries = jax.random.normal(key, shape, jnp.float32) * width
    if len(shards) > 0:
        entries = level_of(key, shape, shards, -0.22, 0.18) * entries
    return jnp.clip(entries, min=-limit, max=limit).astype(held_as)


def setup_inputs(seed: int = 0) -> dict:
    key_of = jax.random.split(jax.random.key(seed), 8)
    return {
        "queries": gaussian(key_of[0], (TOKENS, FEAT), 0.3, 1.75, ((0, 64), (1, 8)), jnp.float32),
        "key_vectors": gaussian(key_of[1], (TOKENS, FEAT), 0.3, 1.75, ((0, 64), (1, 8)), jnp.float32),
        "value_vectors": gaussian(key_of[2], (TOKENS, FEAT), 1.0, 6.0, ((0, 64), (1, 8)), jnp.float32),
        "out_grad": gaussian(key_of[3], (TOKENS, FEAT), 1.0, 6.0, ((0, 64), (1, 8)), jnp.float32),
        "norm_gain": jnp.clip(1.0 + 0.1 * jax.random.normal(key_of[4], (FEAT,), jnp.float32), 0.5, 1.5),
        "decay_rates": jnp.clip(jnp.exp(math.log(0.05) - 11.718964 * jax.random.uniform(key_of[5], (HEADS,), jnp.float32) ** level_of(key_of[5], (HEADS,), ((0, 8),), -0.2, 0.2)), 4.0690105151952594e-07, 0.05),
        "segment_ids": jnp.searchsorted(jnp.cumsum(ragged(key_of[6], SEGS, TOKENS, TOKENS // 3, 0)), jnp.arange(TOKENS), side="right").astype(jnp.int32),
    }


PRECISE = lax.Precision.HIGHEST
EPSILON = 1e-06

def block_tables(segs, rates):
    length = segs.shape[0]
    places = jnp.arange(length, dtype=jnp.float32)
    first_seg = segs[0]
    last_seg = segs[length - 1]
    distance = places[:, None] - places[None, :]
    causal = (distance >= 0.0) & (segs[:, None] == segs[None, :])
    weights = jnp.where(causal[None], jnp.exp(-rates[:, None, None] * jnp.maximum(distance, 0.0)[None]), 0.0)
    head_first = (segs == first_seg).astype(jnp.float32)
    tail_last = (segs == last_seg).astype(jnp.float32)
    carry_in_w = jnp.exp(-rates[None, :] * (places[:, None] + 1.0)) * head_first[:, None]
    carry_out_w = jnp.exp(-rates[None, :] * (length - 1.0 - places[:, None])) * tail_last[:, None]
    back_in = jnp.exp(-rates[None, :] * (length - places[:, None])) * tail_last[:, None]
    back_out = jnp.exp(-rates[None, :] * places[:, None]) * head_first[:, None]
    multiplier = jnp.exp(-rates * length) * (first_seg == last_seg).astype(jnp.float32)
    return (weights, carry_in_w, carry_out_w, back_in, back_out, multiplier)

def reference(queries, key_vectors, value_vectors, out_grad, norm_gain, decay_rates, segment_ids):
    head_count = HEADS
    length = TOK_DEV
    features = HEADS * HEAD_DIM
    query_blocks = queries.reshape(N_SEQ, length, head_count, HEAD_DIM)
    key_blocks = key_vectors.reshape(N_SEQ, length, head_count, HEAD_DIM)
    value_blocks = value_vectors.reshape(N_SEQ, length, head_count, HEAD_DIM)
    grad_blocks = out_grad.reshape(N_SEQ, length, features)
    seg_blocks = segment_ids.reshape(N_SEQ, length)
    zero_state = jnp.zeros((head_count, HEAD_DIM, HEAD_DIM), jnp.float32)

    def forward_step(carry, block):
        prev_state, prev_seg = carry
        query_rows, key_rows, value_rows, grad_rows, segs = block
        weights, carry_in_w, carry_out_w, back_in, back_out, multiplier = block_tables(segs, decay_rates)
        first_seg = segs[0].astype(jnp.float32)
        last_seg = segs[length - 1].astype(jnp.float32)
        carry_in = jnp.where(first_seg == prev_seg, 1.0, 0.0).astype(jnp.float32) * prev_state
        scores = jnp.einsum('ihd,jhd->hij', query_rows, key_rows, precision=PRECISE) * weights
        outputs = jnp.einsum('hij,jhd->ihd', scores, value_rows, precision=PRECISE)
        outputs = outputs + carry_in_w[:, :, None] * jnp.einsum('ihd,hde->ihe', query_rows, carry_in, precision=PRECISE)
        flat_out = outputs.reshape(length, features)
        shaped = grad_rows * norm_gain[None, :]
        squares = lax.optimization_barrier(jnp.sum(flat_out * flat_out, axis=1))
        product = lax.optimization_barrier(jnp.sum(shaped * flat_out, axis=1))
        inv_rms = lax.rsqrt(squares / features + EPSILON)
        coef_rms = inv_rms ** 3 * (product / features)
        grad_flat = inv_rms[:, None] * shaped - coef_rms[:, None] * flat_out
        gain_part = lax.optimization_barrier(jnp.sum(grad_rows * flat_out * inv_rms[:, None], axis=0))
        grad_heads = grad_flat.reshape(length, head_count, HEAD_DIM)
        mixed = jnp.einsum('ihe,jhe->hij', grad_heads, value_rows, precision=PRECISE) * weights
        query_grad = jnp.einsum('hij,jhd->ihd', mixed, key_rows, precision=PRECISE)
        query_grad = query_grad + carry_in_w[:, :, None] * jnp.einsum('ihe,hde->ihd', grad_heads, carry_in, precision=PRECISE)
        state_loc = jnp.einsum('jhd,jhe->hde', key_rows * carry_out_w[:, :, None], value_rows, precision=PRECISE)
        new_state = state_loc + multiplier[:, None, None] * carry_in
        return ((new_state, last_seg), (grad_heads, query_grad.astype(jnp.bfloat16), gain_part))
    start_seg = jnp.array(-1.0, dtype=jnp.float32)
    carry_end, results = lax.scan(forward_step, (zero_state, start_seg), (query_blocks, key_blocks, value_blocks, grad_blocks, seg_blocks))
    grad_store, query_grad_blocks, gain_parts = results

    def reverse_step(carry, block):
        next_state, next_seg = carry
        query_rows, key_rows, value_rows, grad_heads, segs = block
        weights, carry_in_w, carry_out_w, back_in, back_out, multiplier = block_tables(segs, decay_rates)
        first_seg = segs[0].astype(jnp.float32)
        last_seg = segs[length - 1].astype(jnp.float32)
        carry_back = jnp.where(last_seg == next_seg, 1.0, 0.0).astype(jnp.float32) * next_state
        scores = jnp.einsum('ihd,jhd->hij', query_rows, key_rows, precision=PRECISE) * weights
        mixed = jnp.einsum('ihe,jhe->hij', grad_heads, value_rows, precision=PRECISE) * weights
        key_grad = jnp.einsum('hij,ihd->jhd', mixed, query_rows, precision=PRECISE)
        key_grad = key_grad + back_in[:, :, None] * jnp.einsum('jhe,hde->jhd', value_rows, carry_back, precision=PRECISE)
        value_grad = jnp.einsum('hij,ihe->jhe', scores, grad_heads, precision=PRECISE)
        value_grad = value_grad + back_in[:, :, None] * jnp.einsum('jhd,hde->jhe', key_rows, carry_back, precision=PRECISE)
        back_loc = jnp.einsum('thd,the->hde', query_rows * back_out[:, :, None], grad_heads, precision=PRECISE)
        new_state = back_loc + multiplier[:, None, None] * carry_back
        return ((new_state, first_seg), (key_grad.astype(jnp.bfloat16), value_grad.astype(jnp.bfloat16)))
    carry_top, back_results = lax.scan(reverse_step, (zero_state, start_seg), (query_blocks, key_blocks, value_blocks, grad_store, seg_blocks), reverse=True)
    key_grad_blocks, value_grad_blocks = back_results
    gain_grad = lax.optimization_barrier(jnp.sum(gain_parts, axis=0))
    return (query_grad_blocks.reshape(N_SEQ * length, features), key_grad_blocks.reshape(N_SEQ * length, features), value_grad_blocks.reshape(N_SEQ * length, features), gain_grad)
```

```python
import functools
import jax
import jax.numpy as jnp
from jax import lax
from jax.experimental import pallas as pl
from jax.experimental.pallas import tpu as pltpu
from jax.sharding import PartitionSpec as P

F32 = jnp.float32
BF16 = jnp.bfloat16
D = 128
L = 384
NH = 4
G = 8
CH = 64
PR = CH + 8
EPS = 1e-06
PLANES = [[G * z + i for i in range(G)] for z in range(8)]
COLUMNS = [[G * z + i for z in range(8)] for i in range(G)]
SMEM = pltpu.SMEM


def split(x):
    hi = x.astype(BF16)
    return hi, (x - hi.astype(F32)).astype(BF16)


def dot3(a, b, ca, cb):
    dims = (((ca,), (cb,)), ((), ()))
    dg = functools.partial(lax.dot_general, dimension_numbers=dims, preferred_element_type=F32)
    return dg(a[0], b[0]) + (dg(a[0], b[1]) + dg(a[1], b[0]))


def first_at_least(seg_ref, value):
    lo = jnp.int32(0)
    size = jnp.int32(0)
    for step in (256, 128, 64, 32, 16, 8, 4, 2, 1):
        probe = lo + step
        inside = probe <= L
        below = seg_ref[jnp.minimum(probe, L) - 1] < value
        lo = jnp.where(inside & below, probe, lo)
    return lo + size


def rows_iota(n=L):
    return lax.broadcasted_iota(jnp.int32, (n, D), 0)


def seg_of(places, bounds):
    s = jnp.zeros(places.shape, jnp.int32)
    for b in bounds:
        s = s + (places >= b).astype(jnp.int32)
    return s


def notes(first, last, rate):
    row = lax.broadcasted_iota(jnp.int32, (8, D), 0)
    return jnp.where(row == 0, first, jnp.where(row == 1, last, jnp.where(row == 2, rate, 0.0)))


def put_state(out_ref, state, note):
    out_ref[0:CH, :] = state[0:CH]
    out_ref[CH:PR, :] = note
    out_ref[PR : PR + CH, :] = state[CH:]
    out_ref[PR + CH :, :] = note


def k_state(seg_ref, rate_ref, k_ref, v_ref, out_ref):
    h = pl.program_id(0)
    rate = rate_ref[h]
    first, last = seg_ref[0], seg_ref[L - 1]
    start = first_at_least(seg_ref, last)
    i = rows_iota()
    b = jnp.where(i >= start, jnp.exp(-rate * (L - 1 - i).astype(F32)), 0.0)
    u = dot3(split(k_ref[...] * b), split(v_ref[...]), 0, 0)
    put_state(out_ref, u, notes(first.astype(F32), last.astype(F32), rate))


def weights(rate, bounds, rb):
    n = (rb + 1) * D
    i = lax.broadcasted_iota(jnp.int32, (D, n), 0) + rb * D
    j = lax.broadcasted_iota(jnp.int32, (D, n), 1)
    si = seg_of(lax.broadcasted_iota(jnp.int32, (D, 1), 0) + rb * D, bounds)
    sj = seg_of(lax.broadcasted_iota(jnp.int32, (1, n), 1), bounds)
    dist = jnp.maximum(i - j, 0).astype(F32)
    return jnp.where((i >= j) & (si == sj), jnp.exp(-rate * dist), 0.0)


def k_local(seg_ref, rate_ref, q_ref, k_ref, v_ref, o_ref, bnd_ref):
    h = pl.program_id(0)

    @pl.when(h == 0)
    def _():
        for t in range(1, 6):
            bnd_ref[t - 1] = first_at_least(seg_ref, t)
        bnd_ref[5] = first_at_least(seg_ref, seg_ref[0] + 1)
        bnd_ref[6] = first_at_least(seg_ref, seg_ref[L - 1])
        bnd_ref[7] = 0

    bounds = [bnd_ref[t] for t in range(5)]
    rate = rate_ref[h]
    qs, ks, vs = split(q_ref[...]), split(k_ref[...]), split(v_ref[...])
    for rb in range(3):
        n = (rb + 1) * D
        qr = [x[rb * D : n] for x in qs]
        kc = [x[:n] for x in ks]
        vc = [x[:n] for x in vs]
        a = dot3(qr, kc, 1, 1) * weights(rate, bounds, rb)
        o_ref[rb * D : n, :] = dot3(split(a), vc, 1, 0)


def chain(recv_ref, state, reverse, take):
    rate = recv_ref[CH + 2 : CH + 3, :]
    lam = jnp.exp(-rate * float(L))
    order = range(G - 1, -1, -1) if reverse else range(G)
    prev = None
    for i in order:
        base = i * PR
        enter = recv_ref[base + CH + (1 if reverse else 0) : base + CH + (2 if reverse else 1), :]
        leave = recv_ref[base + CH + (0 if reverse else 1) : base + CH + (1 if reverse else 2), :]
        if prev is not None:
            state = jnp.where(prev == enter, 1.0, 0.0) * state
        take(i, state)
        here = recv_ref[base : base + CH, :]
        if state is None:
            state = here
        else:
            state = here + jnp.where(enter == leave, lam, 0.0) * state
        prev = leave
    return state


def k_total(recv_ref, t_ref, *, reverse):
    t_ref[0:CH, :] = chain(recv_ref, jnp.zeros((CH, D), F32), reverse, lambda i, s: None)
    edge = 0 if reverse else G - 1
    t_ref[CH:PR, :] = recv_ref[edge * PR + CH : edge * PR + PR, :]


def k_carry(recv_ref, t1_ref, t2_ref, t3_ref, *rest, reverse):
    out_ref = rest[-1]
    rate = recv_ref[CH + 2 : CH + 3, :]
    edge = G - 1 if reverse else 0
    row = CH + (1 if reverse else 0)
    enter = recv_ref[edge * PR + row : edge * PR + row + 1, :]
    leave = CH + (0 if reverse else 1)
    state = jnp.zeros((CH, D), F32)
    for d, t_ref in enumerate((t1_ref, t2_ref, t3_ref)):
        same = t_ref[leave : leave + 1, :] == enter
        state = state + jnp.where(same, jnp.exp(-rate * float(L * G * d)), 0.0) * t_ref[0:CH, :]
    rows = PR if reverse else CH
    if reverse:
        gain_ref = rest[0]
        gain = gain_ref[0:8, :]
        for z in range(1, 8):
            gain = gain + gain_ref[8 * z : 8 * z + 8, :]

    def take(i, s):
        out_ref[i * rows : i * rows + CH, :] = s
        if reverse:
            out_ref[i * rows + CH : i * rows + PR, :] = gain

    chain(recv_ref, state, reverse, take)


def k_norm(bnd_ref, rate_ref, q_ref, c_ref, ol_ref, og_ref, gain_ref, o_ref, red_ref, sq, pr):
    h = pl.program_id(0)
    rate = rate_ref[h]
    i = rows_iota()
    a = jnp.where(i < bnd_ref[5], jnp.exp(-rate * (i + 1).astype(F32)), 0.0)
    o = ol_ref[...] + a * dot3(split(q_ref[...]), split(c_ref[...]), 1, 0)
    o_ref[...] = o
    g = og_ref[...] * gain_ref[...].reshape(1, D)

    @pl.when(h == 0)
    def _():
        sq[...] = o * o
        pr[...] = g * o

    @pl.when(h > 0)
    def _():
        sq[...] += o * o
        pr[...] += g * o

    @pl.when(h == NH - 1)
    def _():
        ones = jnp.ones((8, D), BF16)
        dims = (((1,), (1,)), ((), ()))
        dg = functools.partial(lax.dot_general, dimension_numbers=dims, preferred_element_type=F32)
        rows = []
        for ref in (sq, pr):
            hi, lo = split(ref[...])
            both = dg(ones, hi) + dg(ones, lo)
            rows += [both[0:1, t * D : (t + 1) * D] for t in range(3)]
        tile = jnp.concatenate(rows + [jnp.zeros((2, D), F32)], axis=0)
        for t in range(8):
            red_ref[8 * t : 8 * t + 8, :] = tile


def k_grad(
    seg_ref, bnd_ref, rate_ref, red_ref, og_ref, o_ref, q_ref, gain_ref,
    do_ref, out_ref, gp_ref, rcol, ccol, gsum,
):
    h = pl.program_id(0)
    rate = rate_ref[h]

    @pl.when(h == 0)
    def _():
        tot = red_ref[0:8, :]
        for t in range(1, 8):
            tot = tot + red_ref[8 * t : 8 * t + 8, :]
        inv = lax.rsqrt(tot[0:3] / 4096.0 + EPS)
        coef = inv * inv * inv * (tot[3:6] / 4096.0)
        for t in range(3):
            rcol[t * D : (t + 1) * D, :] = jnp.broadcast_to(inv[t : t + 1], (D, D)).T
            ccol[t * D : (t + 1) * D, :] = jnp.broadcast_to(coef[t : t + 1], (D, D)).T

    og = og_ref[...]
    o = o_ref[...]
    r = rcol[...]
    do = r * (og * gain_ref[...].reshape(1, D)) - ccol[...] * o
    do_ref[...] = do
    i = rows_iota()
    e = jnp.where(i < bnd_ref[5], jnp.exp(-rate * i.astype(F32)), 0.0)
    v = dot3(split(q_ref[...] * e), split(do), 0, 0)
    put_state(out_ref, v, notes(seg_ref[0].astype(F32), seg_ref[L - 1].astype(F32), rate))
    part = jnp.sum(og * o * r, axis=0, keepdims=True)

    @pl.when(h == 0)
    def _():
        gsum[...] = jnp.zeros_like(gsum)

    row = lax.broadcasted_iota(jnp.int32, (8, D), 0)
    gsum[...] = jnp.where(row == h, part, gsum[...])

    @pl.when(h == NH - 1)
    def _():
        for t in range(8):
            gp_ref[8 * t : 8 * t + 8, :] = gsum[...]


def k_pgrad(bnd_ref, rate_ref, q_ref, k_ref, v_ref, do_ref, c_ref, dq_ref, dk_ref):
    h = pl.program_id(0)
    rate = rate_ref[h]
    bounds = [bnd_ref[t] for t in range(5)]
    qs, ks, vs, ds = [split(x[...]) for x in (q_ref, k_ref, v_ref, do_ref)]
    cs = split(c_ref[...])
    for rb in range(3):
        n = (rb + 1) * D
        rows = slice(rb * D, n)
        dr = [x[rows] for x in ds]
        p = split(dot3(dr, [x[:n] for x in vs], 1, 1) * weights(rate, bounds, rb))
        i = rows_iota(D) + rb * D
        a = jnp.where(i < bnd_ref[5], jnp.exp(-rate * (i + 1).astype(F32)), 0.0)
        dq = dot3(p, [x[:n] for x in ks], 1, 0) + a * dot3(dr, cs, 1, 1)
        dq_ref[rows, :] = dq.astype(BF16)
        part = dot3(p, [x[rows] for x in qs], 0, 0)
        if rb == 0:
            dk_ref[0:n, :] = part
        else:
            dk_ref[0 : n - D, :] += part[: n - D]
            dk_ref[rows, :] = part[n - D :]


def k_vgrad(bnd_ref, rate_ref, q_ref, k_ref, do_ref, dv_ref):
    h = pl.program_id(0)
    rate = rate_ref[h]
    bounds = [bnd_ref[t] for t in range(5)]
    qs, ks, ds = [split(x[...]) for x in (q_ref, k_ref, do_ref)]
    for rb in range(3):
        n = (rb + 1) * D
        rows = slice(rb * D, n)
        s = dot3([x[rows] for x in qs], [x[:n] for x in ks], 1, 1)
        a = split(s * weights(rate, bounds, rb))
        part = dot3(a, [x[rows] for x in ds], 0, 0)
        if rb == 0:
            dv_ref[0:n, :] = part
        else:
            dv_ref[0 : n - D, :] += part[: n - D]
            dv_ref[rows, :] = part[n - D :]


def k_final(bnd_ref, rate_ref, k_ref, v_ref, st_ref, all_ref, dkl_ref, dvl_ref, dk_ref, dv_ref, gg_ref):
    h = pl.program_id(0)
    rate = rate_ref[h]
    i = rows_iota()
    c = jnp.where(i >= bnd_ref[6], jnp.exp(-rate * (L - i).astype(F32)), 0.0)
    state = jnp.concatenate([st_ref[0:CH, :], st_ref[PR : PR + CH, :]], axis=0)
    ss = split(state)
    dk_ref[...] = (dkl_ref[...] + c * dot3(split(v_ref[...]), ss, 1, 1)).astype(BF16)
    dv_ref[...] = (dvl_ref[...] + c * dot3(split(k_ref[...]), ss, 1, 0)).astype(BF16)

    @pl.when(h == 0)
    def _():
        tot = all_ref[CH:PR, :]
        for t in range(1, G):
            tot = tot + all_ref[t * PR + CH : t * PR + PR, :]
        for t in range(NH):
            gg_ref[t * D : (t + 1) * D] = tot[t]


def head_block():
    return pl.BlockSpec((L, D), lambda h: (0, h))


def rows_block(n):
    return pl.BlockSpec((n, D), lambda h: (h, 0))


def gain_block():
    return pl.BlockSpec((D,), lambda h: (h,))


def whole(*shape):
    return pl.BlockSpec(shape, lambda h: (0,) * len(shape))


def scalars():
    return pl.BlockSpec(memory_space=SMEM)


def sds(shape, dtype=F32):
    return jax.ShapeDtypeStruct(shape, dtype)


def heads_call(kernel, in_specs, out_specs, out_shape, flops, scratch=(), name=None):
    return pl.pallas_call(
        kernel,
        grid=(NH,),
        in_specs=in_specs,
        out_specs=out_specs,
        out_shape=out_shape,
        scratch_shapes=list(scratch),
        compiler_params=pltpu.CompilerParams(dimension_semantics=("arbitrary",)),
        cost_estimate=pl.CostEstimate(flops=flops, transcendentals=0, bytes_accessed=3 << 20),
        name=name,
    )


def small_call(kernel, n_in, out_shape, name):
    vm = pl.BlockSpec(memory_space=pltpu.VMEM)
    return pl.pallas_call(
        kernel,
        in_specs=[vm] * n_in,
        out_specs=vm,
        out_shape=out_shape,
        cost_estimate=pl.CostEstimate(flops=1 << 20, transcendentals=0, bytes_accessed=1 << 19),
        name=name,
    )


def exchange(x, axis="seq", groups=PLANES):
    return lax.all_to_all(x, axis, 0, 0, tiled=True, axis_index_groups=groups)


def scan_groups(payload, reverse, extra=()):
    recv = exchange(payload)
    total = small_call(
        functools.partial(k_total, reverse=reverse), 1, sds((PR, D)), "total"
    )(recv)
    n = 64
    sent = []
    for d in (1, 2, 3):
        if reverse:
            perm = [(i, i - G * d) for i in range(G * d, n)]
        else:
            perm = [(i, i + G * d) for i in range(n - G * d)]
        sent.append(lax.ppermute(total, "seq", perm))
    rows = PR if reverse else CH
    back = small_call(
        functools.partial(k_carry, reverse=reverse), 4 + len(extra), sds((G * rows, D)), "carry"
    )(recv, *sent, *extra)
    return exchange(back)


def body(queries, key_vectors, value_vectors, out_grad, norm_gain, decay_rates, segment_ids):
    hb, sc = head_block(), scalars()
    big = 9 * 2 * L * L * D * NH
    flat = sds((L, NH * D))
    payload = heads_call(
        k_state, [sc, sc, hb, hb], rows_block(2 * PR), sds((G * PR, D)), big // 6, name="state"
    )(segment_ids, decay_rates, key_vectors, value_vectors)
    local_out, bnd = heads_call(
        k_local, [sc, sc, hb, hb, hb], [hb, sc], [flat, sds((8,), jnp.int32)], big, name="local"
    )(segment_ids, decay_rates, queries, key_vectors, value_vectors)
    carry = scan_groups(payload, False)
    out, red = heads_call(
        k_norm,
        [sc, sc, hb, rows_block(D), hb, hb, gain_block()],
        [hb, whole(64, D)],
        [flat, sds((64, D))],
        big // 6,
        [pltpu.VMEM((L, D), F32)] * 2,
        name="norm",
    )(bnd, decay_rates, queries, carry, local_out, out_grad, norm_gain)
    sums = exchange(red, "head", None)
    grad_out, payload, gain_part = heads_call(
        k_grad,
        [sc, sc, sc, whole(64, D), hb, hb, hb, gain_block()],
        [hb, rows_block(2 * PR), whole(64, D)],
        [flat, sds((G * PR, D)), sds((64, D))],
        big // 6,
        [pltpu.VMEM((L, D), F32)] * 2 + [pltpu.VMEM((8, D), F32)],
        name="grad",
    )(segment_ids, bnd, decay_rates, sums, out_grad, out, queries, norm_gain)
    gain_all = exchange(gain_part, "seq", COLUMNS)
    dq, dk_local = heads_call(
        k_pgrad,
        [sc, sc, hb, hb, hb, hb, rows_block(D)],
        [hb, hb],
        [sds((L, NH * D), BF16), flat],
        big,
        name="pgrad",
    )(bnd, decay_rates, queries, key_vectors, value_vectors, grad_out, carry)
    dv_local = heads_call(
        k_vgrad, [sc, sc, hb, hb, hb], hb, flat, big // 2, name="vgrad"
    )(bnd, decay_rates, queries, key_vectors, grad_out)
    back = scan_groups(payload, True, (gain_all,))
    dk, dv, gain_grad = heads_call(
        k_final,
        [sc, sc, hb, hb, rows_block(2 * PR), whole(G * PR, D), hb, hb],
        [hb, hb, whole(NH * D)],
        [sds((L, NH * D), BF16), sds((L, NH * D), BF16), sds((NH * D,))],
        big // 6,
        name="final",
    )(bnd, decay_rates, key_vectors, value_vectors, back, back, dk_local, dv_local)
    return dq, dk, dv, gain_grad


def solution(mesh):
    return jax.shard_map(
        body,
        mesh=mesh,
        in_specs=(
            P("seq", "head"),
            P("seq", "head"),
            P("seq", "head"),
            P("seq", "head"),
            P("head"),
            P("head"),
            P("seq"),
        ),
        out_specs=(P("seq", "head"), P("seq", "head"), P("seq", "head"), P("head")),
        check_vma=False,
    )
```

```python
import functools
import jax
import jax.numpy as jnp
from jax import lax
from jax.experimental import pallas as pl
from jax.experimental.pallas import tpu as pltpu
from jax.sharding import PartitionSpec as P

F32 = jnp.float32
BF16 = jnp.bfloat16
D = 128
L = 384
NH = 4
G = 16
NG = 4
PER = 4
CH = 32
PR = CH + 8
EPS = 1e-06
GROUPS = [[G * z + i for i in range(G)] for z in range(NG)]
COLUMNS = [[G * z + i for z in range(NG)] for i in range(G)]
SMEM = pltpu.SMEM
VMEM = 12 << 20


def split(x):
    hi = x.astype(BF16)
    return hi, (x - hi.astype(F32)).astype(BF16)


def dot3(a, b, ca, cb):
    dims = (((ca,), (cb,)), ((), ()))
    dg = functools.partial(lax.dot_general, dimension_numbers=dims, preferred_element_type=F32)
    return dg(a[0], b[0]) + (dg(a[0], b[1]) + dg(a[1], b[0]))


def first_at_least(seg_ref, value):
    lo = jnp.int32(0)
    size = jnp.int32(0)
    for step in (256, 128, 64, 32, 16, 8, 4, 2, 1):
        probe = lo + step
        inside = probe <= L
        below = seg_ref[jnp.minimum(probe, L) - 1] < value
        lo = jnp.where(inside & below, probe, lo)
    return lo + size


def rows_iota(n=L):
    return lax.broadcasted_iota(jnp.int32, (n, D), 0)


def seg_of(places, bounds):
    s = jnp.zeros(places.shape, jnp.int32)
    for b in bounds:
        s = s + (places >= b).astype(jnp.int32)
    return s


def notes(first, last, rate, gain=0.0):
    row = lax.broadcasted_iota(jnp.int32, (8, D), 0)
    rest = jnp.where(row == 2, rate, jnp.where(row == 3, gain, 0.0))
    return jnp.where(row == 0, first, jnp.where(row == 1, last, rest))


def put_state(out_ref, state, note):
    for t in range(PER):
        out_ref[t * PR : t * PR + CH, :] = state[t * CH : (t + 1) * CH]
        out_ref[t * PR + CH : (t + 1) * PR, :] = note


def k_state(seg_ref, rate_ref, k_ref, v_ref, out_ref, start_ref):
    h = pl.program_id(0)
    rate = rate_ref[h]
    first, last = seg_ref[0], seg_ref[L - 1]

    @pl.when(h == 0)
    def _():
        start_ref[0] = first_at_least(seg_ref, last)

    i = rows_iota()
    b = jnp.where(i >= start_ref[0], jnp.exp(-rate * (L - 1 - i).astype(F32)), 0.0)
    u = dot3(split(k_ref[...] * b), split(v_ref[...]), 0, 0)
    put_state(out_ref, u, notes(first.astype(F32), last.astype(F32), rate))


def weights(rate, bounds, rb):
    n = (rb + 1) * D
    i = lax.broadcasted_iota(jnp.int32, (D, n), 0) + rb * D
    j = lax.broadcasted_iota(jnp.int32, (D, n), 1)
    si = seg_of(lax.broadcasted_iota(jnp.int32, (D, 1), 0) + rb * D, bounds)
    sj = seg_of(lax.broadcasted_iota(jnp.int32, (1, n), 1), bounds)
    dist = jnp.maximum(i - j, 0).astype(F32)
    return jnp.where((i >= j) & (si == sj), jnp.exp(-rate * dist), 0.0)


def k_bounds(seg_ref, rate_ref, q_ref, k_ref, v_ref, o_ref, bnd_ref):
    @pl.when(pl.program_id(0) == 0)
    def _():
        for t in range(1, 6):
            bnd_ref[t - 1] = first_at_least(seg_ref, t)
        bnd_ref[5] = first_at_least(seg_ref, seg_ref[0] + 1)
        bnd_ref[6] = first_at_least(seg_ref, seg_ref[L - 1])
        bnd_ref[7] = 0

    k_local(0, bnd_ref, rate_ref, q_ref, k_ref, v_ref, o_ref)


def k_local(start, bnd_ref, rate_ref, q_ref, k_ref, v_ref, *rest):
    o_ref = rest[-1]
    h = pl.program_id(0) + start
    bounds = [bnd_ref[t] for t in range(5)]
    rate = rate_ref[h]
    qs, ks, vs = split(q_ref[...]), split(k_ref[...]), split(v_ref[...])
    for rb in range(3):
        n = (rb + 1) * D
        qr = [x[rb * D : n] for x in qs]
        kc = [x[:n] for x in ks]
        vc = [x[:n] for x in vs]
        a = dot3(qr, kc, 1, 1) * weights(rate, bounds, rb)
        o_ref[rb * D : n, :] = dot3(split(a), vc, 1, 0)


def chain(recv_ref, state, reverse, take):
    rate = recv_ref[CH + 2 : CH + 3, :]
    lam = jnp.exp(-rate * float(L))
    order = range(G - 1, -1, -1) if reverse else range(G)
    prev = None
    for i in order:
        base = i * PR
        enter = recv_ref[base + CH + (1 if reverse else 0) : base + CH + (2 if reverse else 1), :]
        leave = recv_ref[base + CH + (0 if reverse else 1) : base + CH + (1 if reverse else 2), :]
        if prev is not None:
            state = jnp.where(prev == enter, 1.0, 0.0) * state
        take(i, state)
        here = recv_ref[base : base + CH, :]
        if state is None:
            state = here
        else:
            state = here + jnp.where(enter == leave, lam, 0.0) * state
        prev = leave
    return state


def k_total(recv_ref, *rest, reverse):
    t_ref = rest[-1]
    t_ref[0:CH, :] = chain(recv_ref, jnp.zeros((CH, D), F32), reverse, lambda i, s: None)
    note = recv_ref[CH:PR, :]
    row = lax.broadcasted_iota(jnp.int32, (8, D), 0)
    out = jnp.where(row == 1, recv_ref[(G - 1) * PR + CH : G * PR, :], note)
    if reverse:
        for i in range(1, G):
            note = note + recv_ref[i * PR + CH : (i + 1) * PR, :]
        out = jnp.where(row == 3, note, out)
    t_ref[CH:PR, :] = out
    for t in range(1, NG):
        t_ref[t * PR : (t + 1) * PR, :] = t_ref[0:PR, :]


def k_carry(recv_ref, t_ref, *rest, reverse):
    out_ref = rest[-1]
    mine = lax.div(lax.axis_index("seq"), G)
    rate = recv_ref[CH + 2 : CH + 3, :]
    edge = G - 1 if reverse else 0
    row = edge * PR + CH + (1 if reverse else 0)
    enter = recv_ref[row : row + 1, :]
    state = jnp.zeros((CH, D), F32)
    gain = jnp.zeros((8, D), F32)
    for g in range(NG):
        base = g * PR
        leave = base + CH + (0 if reverse else 1)
        gap = (g - 1 - mine) if reverse else (mine - 1 - g)
        same = (t_ref[leave : leave + 1, :] == enter) & (gap >= 0)
        power = jnp.maximum(gap, 0).astype(F32) * float(L * G)
        state = state + jnp.where(same, jnp.exp(-rate * power), 0.0) * t_ref[base : base + CH, :]
        gain = gain + t_ref[base + CH : base + PR, :]
    rows = PR if reverse else CH

    def take(i, s):
        out_ref[i * rows : i * rows + CH, :] = s
        if reverse:
            out_ref[i * rows + CH : i * rows + PR, :] = gain

    chain(recv_ref, state, reverse, take)


def k_norm(bnd_ref, rate_ref, q_ref, c_ref, ol_ref, og_ref, gain_ref, o_ref, red_ref, sq, pr):
    h = pl.program_id(0)
    rate = rate_ref[h]
    i = rows_iota()
    a = jnp.where(i < bnd_ref[5], jnp.exp(-rate * (i + 1).astype(F32)), 0.0)
    o = ol_ref[...] + a * dot3(split(q_ref[...]), split(c_ref[...]), 1, 0)
    o_ref[...] = o
    g = og_ref[...] * gain_ref[...].reshape(1, D)

    @pl.when(h == 0)
    def _():
        sq[...] = o * o
        pr[...] = g * o

    @pl.when(h > 0)
    def _():
        sq[...] += o * o
        pr[...] += g * o

    @pl.when(h == NH - 1)
    def _():
        ones = jnp.ones((8, D), BF16)
        dims = (((1,), (1,)), ((), ()))
        dg = functools.partial(lax.dot_general, dimension_numbers=dims, preferred_element_type=F32)
        rows = []
        for ref in (sq, pr):
            hi, lo = split(ref[...])
            both = dg(ones, hi) + dg(ones, lo)
            rows += [both[0:1, t * D : (t + 1) * D] for t in range(3)]
        tile = jnp.concatenate(rows + [jnp.zeros((2, D), F32)], axis=0)
        for t in range(8):
            red_ref[8 * t : 8 * t + 8, :] = tile


def k_grad(
    seg_ref, bnd_ref, rate_ref, red_ref, og_ref, o_ref, q_ref, gain_ref,
    do_ref, out_ref, rcol, ccol,
):
    h = pl.program_id(0)
    rate = rate_ref[h]

    @pl.when(h == 0)
    def _():
        tot = red_ref[0:8, :]
        for t in range(1, 8):
            tot = tot + red_ref[8 * t : 8 * t + 8, :]
        inv = lax.rsqrt(tot[0:3] / 4096.0 + EPS)
        coef = inv * inv * inv * (tot[3:6] / 4096.0)
        for t in range(3):
            rcol[t * D : (t + 1) * D, :] = jnp.broadcast_to(inv[t : t + 1], (D, D)).T
            ccol[t * D : (t + 1) * D, :] = jnp.broadcast_to(coef[t : t + 1], (D, D)).T

    og = og_ref[...]
    o = o_ref[...]
    r = rcol[...]
    do = r * (og * gain_ref[...].reshape(1, D)) - ccol[...] * o
    do_ref[...] = do
    i = rows_iota()
    e = jnp.where(i < bnd_ref[5], jnp.exp(-rate * i.astype(F32)), 0.0)
    v = dot3(split(q_ref[...] * e), split(do), 0, 0)
    part = jnp.sum(og * o * r, axis=0, keepdims=True)
    put_state(out_ref, v, notes(seg_ref[0].astype(F32), seg_ref[L - 1].astype(F32), rate, part))


def k_pgrad(start, bnd_ref, rate_ref, q_ref, k_ref, v_ref, do_ref, c_ref, *rest):
    dq_ref, dk_ref = rest[2:4] if start else rest[:2]
    h = pl.program_id(0) + start
    if not start:
        rest[2][...] = jnp.zeros((8, D), F32)
    rate = rate_ref[h]
    bounds = [bnd_ref[t] for t in range(5)]
    qs, ks, vs, ds = [split(x[...]) for x in (q_ref, k_ref, v_ref, do_ref)]
    cs = split(c_ref[...])
    for rb in range(3):
        n = (rb + 1) * D
        rows = slice(rb * D, n)
        dr = [x[rows] for x in ds]
        p = split(dot3(dr, [x[:n] for x in vs], 1, 1) * weights(rate, bounds, rb))
        i = rows_iota(D) + rb * D
        a = jnp.where(i < bnd_ref[5], jnp.exp(-rate * (i + 1).astype(F32)), 0.0)
        dq = dot3(p, [x[:n] for x in ks], 1, 0) + a * dot3(dr, cs, 1, 1)
        dq_ref[rows, :] = dq.astype(BF16)
        part = dot3(p, [x[rows] for x in qs], 0, 0)
        if rb == 0:
            dk_ref[0:n, :] = part
        else:
            dk_ref[0 : n - D, :] += part[: n - D]
            dk_ref[rows, :] = part[n - D :]


def k_vgrad(bnd_ref, rate_ref, q_ref, k_ref, do_ref, dv_ref):
    h = pl.program_id(0)
    rate = rate_ref[h]
    bounds = [bnd_ref[t] for t in range(5)]
    qs, ks, ds = [split(x[...]) for x in (q_ref, k_ref, do_ref)]
    for rb in range(3):
        n = (rb + 1) * D
        rows = slice(rb * D, n)
        s = dot3([x[rows] for x in qs], [x[:n] for x in ks], 1, 1)
        a = split(s * weights(rate, bounds, rb))
        part = dot3(a, [x[rows] for x in ds], 0, 0)
        if rb == 0:
            dv_ref[0:n, :] = part
        else:
            dv_ref[0 : n - D, :] += part[: n - D]
            dv_ref[rows, :] = part[n - D :]


def k_final(bnd_ref, rate_ref, k_ref, v_ref, st_ref, dkl_ref, dvl_ref, dk_ref, dv_ref, gg_ref):
    h = pl.program_id(0)
    rate = rate_ref[h]
    i = rows_iota()
    c = jnp.where(i >= bnd_ref[6], jnp.exp(-rate * (L - i).astype(F32)), 0.0)
    state = jnp.concatenate([st_ref[t * PR : t * PR + CH, :] for t in range(PER)], axis=0)
    ss = split(state)
    dk_ref[...] = (dkl_ref[...] + c * dot3(split(v_ref[...]), ss, 1, 1)).astype(BF16)
    dv_ref[...] = (dvl_ref[...] + c * dot3(split(k_ref[...]), ss, 1, 0)).astype(BF16)
    gg_ref[...] = st_ref[CH + 3, :]


def head_block(start=0):
    return pl.BlockSpec((L, D), lambda h: (0, h + start))


def rows_block(n, start=0):
    return pl.BlockSpec((n, D), lambda h: (h + start, 0))


def gain_block():
    return pl.BlockSpec((D,), lambda h: (h,))


def whole(*shape):
    return pl.BlockSpec(shape, lambda h: (0,) * len(shape))


def scalars():
    return pl.BlockSpec(memory_space=SMEM)


def sds(shape, dtype=F32):
    return jax.ShapeDtypeStruct(shape, dtype)


def far(*arrays):
    return [pltpu.with_memory_space_constraint(x, pltpu.HBM) for x in arrays]


def near(*arrays):
    return [pltpu.with_memory_space_constraint(x, pltpu.VMEM) for x in arrays]


def idle():
    return pl.BlockSpec(memory_space=pl.ANY)


def heads_call(kernel, in_specs, out_specs, out_shape, flops, scratch=(), name=None, heads=NH, aliases={}):
    return pl.pallas_call(
        kernel,
        grid=(heads,),
        input_output_aliases=aliases,
        in_specs=in_specs,
        out_specs=out_specs,
        out_shape=out_shape,
        scratch_shapes=list(scratch),
        compiler_params=pltpu.CompilerParams(
            dimension_semantics=("arbitrary",), vmem_limit_bytes=VMEM
        ),
        cost_estimate=pl.CostEstimate(flops=flops, transcendentals=0, bytes_accessed=3 << 20),
        name=name,
    )


def small_call(kernel, n_in, n_idle, out_shape, name):
    vm = pl.BlockSpec(memory_space=pltpu.VMEM)
    return pl.pallas_call(
        kernel,
        in_specs=[vm] * n_in + [idle()] * n_idle,
        out_specs=vm,
        out_shape=out_shape,
        compiler_params=pltpu.CompilerParams(vmem_limit_bytes=VMEM),
        cost_estimate=pl.CostEstimate(flops=1 << 20, transcendentals=0, bytes_accessed=1 << 19),
        name=name,
    )


def exchange(x, axis="seq", groups=GROUPS):
    return lax.all_to_all(x, axis, 0, 0, tiled=True, axis_index_groups=groups)


def scan_in(payload, reverse, order=()):
    recv = exchange(payload)
    total = small_call(
        functools.partial(k_total, reverse=reverse), 1, len(order), sds((NG * PR, D)), "total"
    )(recv, *order)
    return recv, exchange(total, "seq", COLUMNS)


def scan_out(recv, totals, reverse, order=()):
    rows = PR if reverse else CH
    back = small_call(
        functools.partial(k_carry, reverse=reverse), 2, len(order), sds((G * rows, D)), "carry"
    )(recv, totals, *order)
    return exchange(back)


def body(queries, key_vectors, value_vectors, out_grad, norm_gain, decay_rates, segment_ids):
    hb, sc = head_block(), scalars()
    big = 9 * 2 * L * L * D * NH
    flat = pltpu.VMEM((L, NH * D), F32)
    q, k, v, rates, segs = far(queries, key_vectors, value_vectors, decay_rates, segment_ids)
    payload = heads_call(
        k_state,
        [sc, sc, hb, hb],
        rows_block(PER * PR),
        sds((G * PR, D)),
        big // 6,
        [pltpu.SMEM((1,), jnp.int32)],
        name="state",
    )(segs, rates, k, v)
    half = NH // 2
    late = head_block(half)
    local_out, bnd = heads_call(
        k_bounds,
        [sc, sc, hb, hb, hb],
        [hb, sc],
        [flat, pltpu.HBM((8,), jnp.int32)],
        big // 2,
        name="local",
        heads=half,
    )(segs, rates, q, k, v)
    (bnd,) = far(bnd)
    recv, totals = scan_in(payload, False, (bnd,))
    carry = scan_out(recv, totals, False)
    local_out = heads_call(
        functools.partial(k_local, half),
        [sc, sc, late, late, late, idle()],
        late,
        flat,
        big // 2,
        name="local2",
        heads=half,
        aliases={5: 0},
    )(bnd, rates, q, k, v, *near(local_out))
    out, red = heads_call(
        k_norm,
        [sc, sc, hb, rows_block(D), hb, hb, gain_block()],
        [hb, whole(64, D)],
        [flat, sds((64, D))],
        big // 6,
        [pltpu.VMEM((L, D), F32)] * 2,
        name="norm",
    )(bnd, rates, queries, carry, *near(local_out), out_grad, *far(norm_gain))
    sums = exchange(red, "head", None)
    grad_out, payload = heads_call(
        k_grad,
        [sc, sc, sc, whole(64, D), hb, hb, hb, gain_block()],
        [hb, rows_block(PER * PR)],
        [flat, pltpu.HBM((G * PR, D), F32)],
        big // 6,
        [pltpu.VMEM((L, D), F32)] * 2,
        name="grad",
    )(segs, bnd, rates, sums, out_grad, *near(out), queries, *far(norm_gain))
    (grad_out,) = near(grad_out)
    dv_local = heads_call(
        k_vgrad, [sc, sc, hb, hb, hb], hb, flat, big // 2, name="vgrad"
    )(bnd, rates, q, k, grad_out)
    outs = [pltpu.HBM((L, NH * D), BF16), pltpu.HBM((L, NH * D), F32)]
    dq, dk_local, mark = heads_call(
        functools.partial(k_pgrad, 0),
        [sc, sc, hb, hb, hb, hb, rows_block(D)],
        [hb, hb, whole(8, D)],
        outs + [sds((8, D))],
        big // 2,
        name="pgrad",
        heads=half,
    )(bnd, rates, q, k, v, grad_out, carry)
    recv, totals = scan_in(payload, True, (dv_local,))
    back = scan_out(recv, totals, True, (mark,))
    dq, dk_local = heads_call(
        functools.partial(k_pgrad, half),
        [sc, sc, late, late, late, late, rows_block(D, half), idle(), idle()],
        [late, late],
        outs,
        big // 2,
        name="pgrad2",
        heads=half,
        aliases={7: 0, 8: 1},
    )(bnd, rates, q, k, v, grad_out, carry, *far(dq, dk_local))
    dk, dv, gain_grad = heads_call(
        k_final,
        [sc, sc, hb, hb, rows_block(PER * PR), hb, hb],
        [hb, hb, gain_block()],
        [sds((L, NH * D), BF16), sds((L, NH * D), BF16), sds((NH * D,))],
        big // 6,
        name="final",
    )(bnd, rates, key_vectors, value_vectors, back, *far(dk_local), *near(dv_local))
    return dq, dk, dv, gain_grad


def solution(mesh):
    return jax.shard_map(
        body,
        mesh=mesh,
        in_specs=(
            P("seq", "head"),
            P("seq", "head"),
            P("seq", "head"),
            P("seq", "head"),
            P("head"),
            P("head"),
            P("seq"),
        ),
        out_specs=(P("seq", "head"), P("seq", "head"), P("seq", "head"), P("head")),
        check_vma=False,
    )
```

```python
import functools
import jax
import jax.numpy as jnp
from jax import lax
from jax.experimental import pallas as pl
from jax.experimental.pallas import tpu as pltpu
from jax.sharding import PartitionSpec as P

F32 = jnp.float32
BF16 = jnp.bfloat16
D = 128
L = 384
NH = 4
G = 16
NG = 4
PER = 4
CH = 32
PR = CH + 8
EPS = 1e-06
GROUPS = [[G * z + i for i in range(G)] for z in range(NG)]
COLUMNS = [[G * z + i for z in range(NG)] for i in range(G)]
SMEM = pltpu.SMEM
VMEM = 12 << 20


def split(x):
    hi = x.astype(BF16)
    return hi, (x - hi.astype(F32)).astype(BF16)


def dot3(a, b, ca, cb):
    dims = (((ca,), (cb,)), ((), ()))
    dg = functools.partial(lax.dot_general, dimension_numbers=dims, preferred_element_type=F32)
    return dg(a[0], b[0]) + (dg(a[0], b[1]) + dg(a[1], b[0]))


def first_at_least(seg_ref, value):
    lo = jnp.int32(0)
    size = jnp.int32(0)
    for step in (256, 128, 64, 32, 16, 8, 4, 2, 1):
        probe = lo + step
        inside = probe <= L
        below = seg_ref[jnp.minimum(probe, L) - 1] < value
        lo = jnp.where(inside & below, probe, lo)
    return lo + size


def rows_iota(n=L):
    return lax.broadcasted_iota(jnp.int32, (n, D), 0)


def seg_of(places, bounds):
    s = jnp.zeros(places.shape, jnp.int32)
    for b in bounds:
        s = s + (places >= b).astype(jnp.int32)
    return s


def notes(first, last, rate, gain=0.0):
    row = lax.broadcasted_iota(jnp.int32, (8, D), 0)
    rest = jnp.where(row == 2, rate, jnp.where(row == 3, gain, 0.0))
    return jnp.where(row == 0, first, jnp.where(row == 1, last, rest))


def put_state(out_ref, h, state, note):
    for t in range(PER):
        base = (h * PER + t) * PR
        out_ref[base : base + CH, :] = state[t * CH : (t + 1) * CH]
        out_ref[base + CH : base + PR, :] = note


def head(h):
    return slice(h * D, (h + 1) * D)


def k_state(seg_ref, rate_ref, k_hbm, v_hbm, out_ref, k_ref, v_ref, sems):
    copies = []
    for h in range(NH):
        for t, (src, dst) in enumerate(((k_hbm, k_ref), (v_hbm, v_ref))):
            copies.append(
                pltpu.make_async_copy(src.at[:, head(h)], dst.at[:, head(h)], sems.at[2 * h + t])
            )
            copies[-1].start()
    first, last = seg_ref[0], seg_ref[L - 1]
    start = first_at_least(seg_ref, last)
    i = rows_iota()
    back = (L - 1 - i).astype(F32)
    for h in range(NH):
        rate = rate_ref[h]
        b = jnp.where(i >= start, jnp.exp(-rate * back), 0.0)
        copies[2 * h].wait()
        copies[2 * h + 1].wait()
        u = dot3(split(k_ref[:, head(h)] * b), split(v_ref[:, head(h)]), 0, 0)
        note = notes(first.astype(F32), last.astype(F32), rate)
        put_state(out_ref, h, u, note)


def weights(rate, bounds, rb):
    n = (rb + 1) * D
    i = lax.broadcasted_iota(jnp.int32, (D, n), 0) + rb * D
    j = lax.broadcasted_iota(jnp.int32, (D, n), 1)
    si = seg_of(lax.broadcasted_iota(jnp.int32, (D, 1), 0) + rb * D, bounds)
    sj = seg_of(lax.broadcasted_iota(jnp.int32, (1, n), 1), bounds)
    dist = jnp.maximum(i - j, 0).astype(F32)
    return jnp.where((i >= j) & (si == sj), jnp.exp(-rate * dist), 0.0)


def k_local(seg_ref, rate_ref, q_ref, k_ref, v_ref, gain_ref, o_ref, bnd_ref, con_ref):
    h = pl.program_id(0)

    @pl.when(h == 0)
    def _():
        for t in range(1, 6):
            bnd_ref[t - 1] = first_at_least(seg_ref, t)
        bnd_ref[5] = first_at_least(seg_ref, seg_ref[0] + 1)
        bnd_ref[6] = first_at_least(seg_ref, seg_ref[L - 1])
        bnd_ref[7] = 0
        row = lax.broadcasted_iota(jnp.int32, (8, D), 0)
        tile = jnp.zeros((8, D), F32)
        values = [rate_ref[t] for t in range(NH)]
        values += [bnd_ref[5], bnd_ref[6], seg_ref[0], seg_ref[L - 1]]
        for t, value in enumerate(values):
            tile = jnp.where(row == t, value.astype(F32), tile)
        con_ref[0:8, :] = tile
        for t in range(NH):
            con_ref[8 + t : 9 + t, :] = gain_ref[head(t)].reshape(1, D)
        con_ref[12:16, :] = jnp.zeros((4, D), F32)

    bounds = [bnd_ref[t] for t in range(5)]
    rate = rate_ref[h]
    qs, ks, vs = split(q_ref[...]), split(k_ref[...]), split(v_ref[...])
    for rb in range(3):
        n = (rb + 1) * D
        qr = [x[rb * D : n] for x in qs]
        kc = [x[:n] for x in ks]
        vc = [x[:n] for x in vs]
        a = dot3(qr, kc, 1, 1) * weights(rate, bounds, rb)
        o_ref[rb * D : n, :] = dot3(split(a), vc, 1, 0)


def chain(recv_ref, state, reverse, take):
    rate = recv_ref[CH + 2 : CH + 3, :]
    lam = jnp.exp(-rate * float(L))
    order = range(G - 1, -1, -1) if reverse else range(G)
    prev = None
    for i in order:
        base = i * PR
        enter = recv_ref[base + CH + (1 if reverse else 0) : base + CH + (2 if reverse else 1), :]
        leave = recv_ref[base + CH + (0 if reverse else 1) : base + CH + (1 if reverse else 2), :]
        if prev is not None:
            state = jnp.where(prev == enter, 1.0, 0.0) * state
        take(i, state)
        here = recv_ref[base : base + CH, :]
        if state is None:
            state = here
        else:
            state = here + jnp.where(enter == leave, lam, 0.0) * state
        prev = leave
    return state


def k_total(recv_ref, *rest, reverse):
    t_ref = rest[-1]
    t_ref[0:CH, :] = chain(recv_ref, jnp.zeros((CH, D), F32), reverse, lambda i, s: None)
    note = recv_ref[CH:PR, :]
    row = lax.broadcasted_iota(jnp.int32, (8, D), 0)
    out = jnp.where(row == 1, recv_ref[(G - 1) * PR + CH : G * PR, :], note)
    if reverse:
        for i in range(1, G):
            note = note + recv_ref[i * PR + CH : (i + 1) * PR, :]
        out = jnp.where(row == 3, note, out)
    t_ref[CH:PR, :] = out
    for t in range(1, NG):
        t_ref[t * PR : (t + 1) * PR, :] = t_ref[0:PR, :]


def k_carry(recv_ref, t_ref, *rest, reverse):
    out_ref = rest[-1]
    mine = lax.div(lax.axis_index("seq"), G)
    rate = recv_ref[CH + 2 : CH + 3, :]
    edge = G - 1 if reverse else 0
    row = edge * PR + CH + (1 if reverse else 0)
    enter = recv_ref[row : row + 1, :]
    state = jnp.zeros((CH, D), F32)
    gain = jnp.zeros((8, D), F32)
    for g in range(NG):
        base = g * PR
        leave = base + CH + (0 if reverse else 1)
        gap = (g - 1 - mine) if reverse else (mine - 1 - g)
        same = (t_ref[leave : leave + 1, :] == enter) & (gap >= 0)
        power = jnp.maximum(gap, 0).astype(F32) * float(L * G)
        state = state + jnp.where(same, jnp.exp(-rate * power), 0.0) * t_ref[base : base + CH, :]
        gain = gain + t_ref[base + CH : base + PR, :]
    rows = PR if reverse else CH

    def take(i, s):
        out_ref[i * rows : i * rows + CH, :] = s
        if reverse:
            out_ref[i * rows + CH : i * rows + PR, :] = gain

    chain(recv_ref, state, reverse, take)


def k_norm(con_ref, q_ref, c_ref, ol_ref, og_ref, o_ref, red_ref):
    i = rows_iota().astype(F32)
    ahead = i + 1.0
    inside = i < con_ref[4:5, :]
    sq = pr = None
    for h in range(NH):
        a = jnp.where(inside, jnp.exp(-con_ref[h : h + 1, :] * ahead), 0.0)
        o = ol_ref[:, head(h)] + a * dot3(split(q_ref[:, head(h)]), split(c_ref[head(h), :]), 1, 0)
        o_ref[:, head(h)] = o
        g = og_ref[:, head(h)] * con_ref[8 + h : 9 + h, :]
        sq = o * o if h == 0 else sq + o * o
        pr = g * o if h == 0 else pr + g * o
    ones = jnp.ones((8, D), BF16)
    dims = (((1,), (1,)), ((), ()))
    dg = functools.partial(lax.dot_general, dimension_numbers=dims, preferred_element_type=F32)
    rows = []
    for x in (sq, pr):
        hi, lo = split(x)
        both = dg(ones, hi) + dg(ones, lo)
        rows += [both[0:1, head(t)] for t in range(3)]
    tile = jnp.concatenate(rows + [jnp.zeros((2, D), F32)], axis=0)
    for t in range(8):
        red_ref[8 * t : 8 * t + 8, :] = tile


def k_grad(
    con_ref, red_ref, og_ref, o_ref, q_ref, do_ref, out_ref
):
    tot = red_ref[0:8, :]
    for t in range(1, 8):
        tot = tot + red_ref[8 * t : 8 * t + 8, :]
    inv = lax.rsqrt(tot[0:3] / 4096.0 + EPS)
    coef = inv * inv * inv * (tot[3:6] / 4096.0)
    cols = []
    for x in (inv, coef):
        parts = [jnp.broadcast_to(x[t : t + 1], (D, D)).T for t in range(3)]
        cols.append(jnp.concatenate(parts, axis=0))
    r, c = cols
    i = rows_iota().astype(F32)
    inside = i < con_ref[4:5, :]
    first, last = con_ref[6:7, :], con_ref[7:8, :]
    for h in range(NH):
        rate = con_ref[h : h + 1, :]
        rog = r * og_ref[:, head(h)]
        o = o_ref[:, head(h)]
        do = rog * con_ref[8 + h : 9 + h, :] - c * o
        do_ref[:, head(h)] = do
        e = jnp.where(inside, jnp.exp(-rate * i), 0.0)
        v = dot3(split(q_ref[:, head(h)] * e), split(do), 0, 0)
        part = jnp.sum(rog * o, axis=0, keepdims=True)
        put_state(out_ref, h, v, notes(first, last, rate, part))


def k_pgrad(bnd_ref, rate_ref, q_ref, k_ref, v_ref, do_ref, c_ref, dq_ref, dk_ref):
    h = pl.program_id(0)
    rate = rate_ref[h]
    bounds = [bnd_ref[t] for t in range(5)]
    qs, ks, vs, ds = [split(x[...]) for x in (q_ref, k_ref, v_ref, do_ref)]
    cs = split(c_ref[...])
    for rb in range(3):
        n = (rb + 1) * D
        rows = slice(rb * D, n)
        dr = [x[rows] for x in ds]
        p = split(dot3(dr, [x[:n] for x in vs], 1, 1) * weights(rate, bounds, rb))
        i = rows_iota(D) + rb * D
        a = jnp.where(i < bnd_ref[5], jnp.exp(-rate * (i + 1).astype(F32)), 0.0)
        dq = dot3(p, [x[:n] for x in ks], 1, 0) + a * dot3(dr, cs, 1, 1)
        dq_ref[rows, :] = dq.astype(BF16)
        part = dot3(p, [x[rows] for x in qs], 0, 0)
        if rb == 0:
            dk_ref[0:n, :] = part
        else:
            dk_ref[0 : n - D, :] += part[: n - D]
            dk_ref[rows, :] = part[n - D :]


def k_vgrad(bnd_ref, rate_ref, q_ref, k_ref, do_ref, dv_ref):
    h = pl.program_id(0)
    rate = rate_ref[h]
    bounds = [bnd_ref[t] for t in range(5)]
    qs, ks, ds = [split(x[...]) for x in (q_ref, k_ref, do_ref)]
    for rb in range(3):
        n = (rb + 1) * D
        rows = slice(rb * D, n)
        s = dot3([x[rows] for x in qs], [x[:n] for x in ks], 1, 1)
        a = split(s * weights(rate, bounds, rb))
        part = dot3(a, [x[rows] for x in ds], 0, 0)
        if rb == 0:
            dv_ref[0:n, :] = part
        else:
            dv_ref[0 : n - D, :] += part[: n - D]
            dv_ref[rows, :] = part[n - D :]


def k_final(
    con_ref, k_ref, v_ref, st_ref, dkl_hbm, dvl_ref, dk_hbm, dv_hbm, gg_ref,
    dkl_ref, dk_ref, dv_ref, sems,
):
    loads, stores = [], []
    for h in range(NH):
        loads.append(
            pltpu.make_async_copy(dkl_hbm.at[:, head(h)], dkl_ref.at[:, head(h)], sems.at[h])
        )
        loads[-1].start()
    i = rows_iota().astype(F32)
    inside = i >= con_ref[5:6, :]
    back = float(L) - i
    for h in range(NH):
        c = jnp.where(inside, jnp.exp(-con_ref[h : h + 1, :] * back), 0.0)
        bases = [(h * PER + t) * PR for t in range(PER)]
        ss = split(jnp.concatenate([st_ref[b : b + CH, :] for b in bases], axis=0))
        gg_ref[head(h)] = st_ref[bases[0] + CH + 3, :]
        for t in range(2):
            if t == 0:
                x = dvl_ref[:, head(h)] + c * dot3(split(k_ref[:, head(h)]), ss, 1, 0)
                buf, far_ref = dv_ref, dv_hbm
            else:
                loads[h].wait()
                x = dkl_ref[:, head(h)] + c * dot3(split(v_ref[:, head(h)]), ss, 1, 1)
                buf, far_ref = dk_ref, dk_hbm
            buf[:, head(h)] = x.astype(BF16)
            stores.append(
                pltpu.make_async_copy(
                    buf.at[:, head(h)], far_ref.at[:, head(h)], sems.at[NH + 2 * h + t]
                )
            )
            stores[-1].start()
    for copy in stores:
        copy.wait()


def head_block():
    return pl.BlockSpec((L, D), lambda h: (0, h))


def rows_block(n):
    return pl.BlockSpec((n, D), lambda h: (h, 0))


def whole(*shape):
    return pl.BlockSpec(shape, lambda h: (0,) * len(shape))


def scalars():
    return pl.BlockSpec(memory_space=SMEM)


def sds(shape, dtype=F32):
    return jax.ShapeDtypeStruct(shape, dtype)


def far(*arrays):
    return [pltpu.with_memory_space_constraint(x, pltpu.HBM) for x in arrays]


def near(*arrays):
    return [pltpu.with_memory_space_constraint(x, pltpu.VMEM) for x in arrays]


def idle():
    return pl.BlockSpec(memory_space=pl.ANY)


def heads_call(kernel, in_specs, out_specs, out_shape, flops, scratch=(), name=None):
    return pl.pallas_call(
        kernel,
        grid=(NH,),
        in_specs=in_specs,
        out_specs=out_specs,
        out_shape=out_shape,
        scratch_shapes=list(scratch),
        compiler_params=pltpu.CompilerParams(
            dimension_semantics=("arbitrary",), vmem_limit_bytes=VMEM
        ),
        cost_estimate=pl.CostEstimate(flops=flops, transcendentals=0, bytes_accessed=3 << 20),
        name=name,
    )


def near_block():
    return pl.BlockSpec(memory_space=pltpu.VMEM)


def one_call(kernel, in_specs, out_specs, out_shape, name, flops=1 << 20, scratch=()):
    return pl.pallas_call(
        kernel,
        in_specs=in_specs,
        out_specs=out_specs,
        out_shape=out_shape,
        scratch_shapes=list(scratch),
        compiler_params=pltpu.CompilerParams(vmem_limit_bytes=VMEM),
        cost_estimate=pl.CostEstimate(flops=flops, transcendentals=0, bytes_accessed=1 << 19),
        name=name,
    )


def small_call(kernel, n_in, n_idle, out_shape, name):
    vm = near_block()
    return one_call(kernel, [vm] * n_in + [idle()] * n_idle, vm, out_shape, name)


def exchange(x, axis="seq", groups=GROUPS):
    return lax.all_to_all(x, axis, 0, 0, tiled=True, axis_index_groups=groups)


def scan_groups(payload, reverse, first=(), second=()):
    recv = exchange(payload)
    total = small_call(
        functools.partial(k_total, reverse=reverse), 1, len(first), sds((NG * PR, D)), "total"
    )(recv, *first)
    totals = exchange(total, "seq", COLUMNS)
    rows = PR if reverse else CH
    back = small_call(
        functools.partial(k_carry, reverse=reverse), 2, len(second), sds((G * rows, D)), "carry"
    )(recv, totals, *second)
    return exchange(back)


def body(queries, key_vectors, value_vectors, out_grad, norm_gain, decay_rates, segment_ids):
    hb, sc = head_block(), scalars()
    big = 9 * 2 * L * L * D * NH
    flat = pltpu.VMEM((L, NH * D), F32)
    q, k, v, rates, segs = far(queries, key_vectors, value_vectors, decay_rates, segment_ids)
    vm, work = near_block(), idle()
    payload = one_call(
        k_state,
        [sc, sc, work, work],
        vm,
        sds((G * PR, D)),
        "state",
        big // 6,
        [pltpu.VMEM((L, NH * D), F32)] * 2 + [pltpu.SemaphoreType.DMA((2 * NH,))],
    )(segs, rates, k, v)
    local_out, bnd, con = heads_call(
        k_local,
        [sc, sc, hb, hb, hb, whole(NH * D)],
        [hb, sc, whole(16, D)],
        [flat, pltpu.HBM((8,), jnp.int32), pltpu.VMEM((16, D), F32)],
        big,
        name="local",
    )(segs, rates, q, k, v, *far(norm_gain))
    (bnd,) = far(bnd)
    (con,) = near(con)
    carry = scan_groups(payload, False)
    out, red = one_call(
        k_norm, [vm] * 5, [vm, vm], [flat, sds((64, D))], "norm", big // 6
    )(con, queries, carry, *near(local_out), out_grad)
    sums = exchange(red, "head", None)
    grad_out, payload = one_call(
        k_grad,
        [vm] * 5,
        [vm, vm],
        [flat, sds((G * PR, D))],
        "grad",
        big // 6,
    )(con, sums, out_grad, *near(out), queries)
    (grad_out,) = near(grad_out)
    dq, dk_local = heads_call(
        k_pgrad,
        [sc, sc, hb, hb, hb, hb, rows_block(D)],
        [hb, hb],
        [pltpu.HBM((L, NH * D), BF16), pltpu.HBM((L, NH * D), F32)],
        big,
        name="pgrad",
    )(bnd, rates, q, k, v, *far(grad_out), carry)
    dv_local = heads_call(
        k_vgrad, [sc, sc, hb, hb, hb], hb, flat, big // 2, name="vgrad"
    )(bnd, rates, q, k, grad_out)
    back = scan_groups(payload, True, (dv_local,))
    dk, dv, gain_grad = one_call(
        k_final,
        [vm, vm, vm, vm, work, vm],
        [work, work, vm],
        [pltpu.HBM((L, NH * D), BF16)] * 2 + [sds((NH * D,))],
        "final",
        big // 6,
        [pltpu.VMEM((L, NH * D), t) for t in (F32, BF16, BF16)]
        + [pltpu.SemaphoreType.DMA((3 * NH,))],
    )(con, key_vectors, value_vectors, back, *far(dk_local), *near(dv_local))
    return dq, dk, dv, gain_grad


def solution(mesh):
    return jax.shard_map(
        body,
        mesh=mesh,
        in_specs=(
            P("seq", "head"),
            P("seq", "head"),
            P("seq", "head"),
            P("seq", "head"),
            P("head"),
            P("head"),
            P("seq"),
        ),
        out_specs=(P("seq", "head"), P("seq", "head"), P("seq", "head"), P("head")),
        check_vma=False,
    )
```

```python
import functools
import jax
import jax.numpy as jnp
from jax import lax
from jax.experimental import pallas as pl
from jax.experimental.pallas import tpu as pltpu
from jax.sharding import PartitionSpec as P

F32 = jnp.float32
BF16 = jnp.bfloat16
D = 128
L = 384
NH = 4
G = 16
NG = 4
PER = 4
CH = 32
PR = CH + 8
EPS = 1e-06
GROUPS = [[G * z + i for i in range(G)] for z in range(NG)]
COLUMNS = [[G * z + i for z in range(NG)] for i in range(G)]
SMEM = pltpu.SMEM
VMEM = 12 << 20


def split(x):
    hi = x.astype(BF16)
    return hi, (x - hi.astype(F32)).astype(BF16)


def dot3(a, b, ca, cb):
    dims = (((ca,), (cb,)), ((), ()))
    dg = functools.partial(lax.dot_general, dimension_numbers=dims, preferred_element_type=F32)
    return dg(a[0], b[0]) + (dg(a[0], b[1]) + dg(a[1], b[0]))


def first_at_least(seg_ref, value):
    lo = jnp.int32(0)
    size = jnp.int32(0)
    for step in (256, 128, 64, 32, 16, 8, 4, 2, 1):
        probe = lo + step
        inside = probe <= L
        below = seg_ref[jnp.minimum(probe, L) - 1] < value
        lo = jnp.where(inside & below, probe, lo)
    return lo + size


def rows_iota(n=L):
    return lax.broadcasted_iota(jnp.int32, (n, D), 0)


def seg_of(places, bounds):
    s = jnp.zeros(places.shape, jnp.int32)
    for b in bounds:
        s = s + (places >= b).astype(jnp.int32)
    return s


def notes(first, last, rate, gain=0.0):
    row = lax.broadcasted_iota(jnp.int32, (8, D), 0)
    rest = jnp.where(row == 2, rate, jnp.where(row == 3, gain, 0.0))
    return jnp.where(row == 0, first, jnp.where(row == 1, last, rest))


def put_state(out_ref, h, state, note):
    for t in range(PER):
        base = (h * PER + t) * PR
        out_ref[base : base + CH, :] = state[t * CH : (t + 1) * CH]
        out_ref[base + CH : base + PR, :] = note


def head(h):
    return slice(h * D, (h + 1) * D)


def k_state(seg_hbm, rate_hbm, k_hbm, v_hbm, out_ref, k_ref, v_ref, seg_ref, rate_ref, sems):
    small = [
        pltpu.make_async_copy(seg_hbm, seg_ref, sems.at[2 * NH]),
        pltpu.make_async_copy(rate_hbm, rate_ref, sems.at[2 * NH + 1]),
    ]
    for copy in small:
        copy.start()
    copies = []
    for h in range(NH):
        for t, (src, dst) in enumerate(((k_hbm, k_ref), (v_hbm, v_ref))):
            copies.append(
                pltpu.make_async_copy(src.at[:, head(h)], dst.at[:, head(h)], sems.at[2 * h + t])
            )
            copies[-1].start()
    for copy in small:
        copy.wait()
    first, last = seg_ref[0], seg_ref[L - 1]
    start = first_at_least(seg_ref, last)
    i = rows_iota()
    back = (L - 1 - i).astype(F32)
    for h in range(NH):
        rate = rate_ref[h]
        b = jnp.where(i >= start, jnp.exp(-rate * back), 0.0)
        copies[2 * h].wait()
        copies[2 * h + 1].wait()
        u = dot3(split(k_ref[:, head(h)] * b), split(v_ref[:, head(h)]), 0, 0)
        note = notes(first.astype(F32), last.astype(F32), rate)
        put_state(out_ref, h, u, note)


def weights(rate, bounds, rb):
    n = (rb + 1) * D
    i = lax.broadcasted_iota(jnp.int32, (D, n), 0) + rb * D
    j = lax.broadcasted_iota(jnp.int32, (D, n), 1)
    si = seg_of(lax.broadcasted_iota(jnp.int32, (D, 1), 0) + rb * D, bounds)
    sj = seg_of(lax.broadcasted_iota(jnp.int32, (1, n), 1), bounds)
    dist = jnp.maximum(i - j, 0).astype(F32)
    return jnp.where((i >= j) & (si == sj), jnp.exp(-rate * dist), 0.0)


def k_local(seg_ref, rate_ref, q_ref, k_ref, v_ref, gain_ref, o_ref, bnd_ref, con_ref):
    h = pl.program_id(0)

    @pl.when(h == 0)
    def _():
        for t in range(1, 6):
            bnd_ref[t - 1] = first_at_least(seg_ref, t)
        bnd_ref[5] = first_at_least(seg_ref, seg_ref[0] + 1)
        bnd_ref[6] = first_at_least(seg_ref, seg_ref[L - 1])
        bnd_ref[7] = 0
        row = lax.broadcasted_iota(jnp.int32, (8, D), 0)
        tile = jnp.zeros((8, D), F32)
        values = [rate_ref[t] for t in range(NH)]
        values += [bnd_ref[5], bnd_ref[6], seg_ref[0], seg_ref[L - 1]]
        for t, value in enumerate(values):
            tile = jnp.where(row == t, value.astype(F32), tile)
        con_ref[0:8, :] = tile
        for t in range(NH):
            con_ref[8 + t : 9 + t, :] = gain_ref[head(t)].reshape(1, D)
        con_ref[12:16, :] = jnp.zeros((4, D), F32)

    bounds = [bnd_ref[t] for t in range(5)]
    rate = rate_ref[h]
    qs, ks, vs = split(q_ref[...]), split(k_ref[...]), split(v_ref[...])
    for rb in range(3):
        n = (rb + 1) * D
        qr = [x[rb * D : n] for x in qs]
        kc = [x[:n] for x in ks]
        vc = [x[:n] for x in vs]
        a = dot3(qr, kc, 1, 1) * weights(rate, bounds, rb)
        o_ref[rb * D : n, :] = dot3(split(a), vc, 1, 0)


def chain(recv_ref, state, reverse, take):
    rate = recv_ref[CH + 2 : CH + 3, :]
    lam = jnp.exp(-rate * float(L))
    order = range(G - 1, -1, -1) if reverse else range(G)
    prev = None
    for i in order:
        base = i * PR
        enter = recv_ref[base + CH + (1 if reverse else 0) : base + CH + (2 if reverse else 1), :]
        leave = recv_ref[base + CH + (0 if reverse else 1) : base + CH + (1 if reverse else 2), :]
        if prev is not None:
            state = jnp.where(prev == enter, 1.0, 0.0) * state
        take(i, state)
        here = recv_ref[base : base + CH, :]
        if state is None:
            state = here
        else:
            state = here + jnp.where(enter == leave, lam, 0.0) * state
        prev = leave
    return state


def k_total(recv_ref, *rest, reverse):
    t_ref = rest[-1]
    t_ref[0:CH, :] = chain(recv_ref, jnp.zeros((CH, D), F32), reverse, lambda i, s: None)
    note = recv_ref[CH:PR, :]
    row = lax.broadcasted_iota(jnp.int32, (8, D), 0)
    out = jnp.where(row == 1, recv_ref[(G - 1) * PR + CH : G * PR, :], note)
    if reverse:
        for i in range(1, G):
            note = note + recv_ref[i * PR + CH : (i + 1) * PR, :]
        out = jnp.where(row == 3, note, out)
    t_ref[CH:PR, :] = out
    for t in range(1, NG):
        t_ref[t * PR : (t + 1) * PR, :] = t_ref[0:PR, :]


def k_carry(recv_ref, t_ref, *rest, reverse):
    out_ref = rest[-1]
    mine = lax.div(lax.axis_index("seq"), G)
    rate = recv_ref[CH + 2 : CH + 3, :]
    edge = G - 1 if reverse else 0
    row = edge * PR + CH + (1 if reverse else 0)
    enter = recv_ref[row : row + 1, :]
    state = jnp.zeros((CH, D), F32)
    gain = jnp.zeros((8, D), F32)
    for g in range(NG):
        base = g * PR
        leave = base + CH + (0 if reverse else 1)
        gap = (g - 1 - mine) if reverse else (mine - 1 - g)
        same = (t_ref[leave : leave + 1, :] == enter) & (gap >= 0)
        power = jnp.maximum(gap, 0).astype(F32) * float(L * G)
        state = state + jnp.where(same, jnp.exp(-rate * power), 0.0) * t_ref[base : base + CH, :]
        gain = gain + t_ref[base + CH : base + PR, :]
    rows = PR if reverse else CH

    def take(i, s):
        out_ref[i * rows : i * rows + CH, :] = s
        if reverse:
            out_ref[i * rows + CH : i * rows + PR, :] = gain

    chain(recv_ref, state, reverse, take)


def k_norm(con_ref, q_ref, c_ref, ol_ref, og_ref, o_ref, red_ref):
    i = rows_iota().astype(F32)
    ahead = i + 1.0
    inside = i < con_ref[4:5, :]
    sq = pr = None
    for h in range(NH):
        a = jnp.where(inside, jnp.exp(-con_ref[h : h + 1, :] * ahead), 0.0)
        o = ol_ref[:, head(h)] + a * dot3(split(q_ref[:, head(h)]), split(c_ref[head(h), :]), 1, 0)
        o_ref[:, head(h)] = o
        g = og_ref[:, head(h)] * con_ref[8 + h : 9 + h, :]
        sq = o * o if h == 0 else sq + o * o
        pr = g * o if h == 0 else pr + g * o
    ones = jnp.ones((8, D), BF16)
    dims = (((1,), (1,)), ((), ()))
    dg = functools.partial(lax.dot_general, dimension_numbers=dims, preferred_element_type=F32)
    rows = []
    for x in (sq, pr):
        hi, lo = split(x)
        both = dg(ones, hi) + dg(ones, lo)
        rows += [both[0:1, head(t)] for t in range(3)]
    tile = jnp.concatenate(rows + [jnp.zeros((2, D), F32)], axis=0)
    for t in range(8):
        red_ref[8 * t : 8 * t + 8, :] = tile


def k_grad(
    con_ref, red_ref, og_ref, o_ref, q_ref, do_ref, out_ref
):
    tot = red_ref[0:8, :]
    for t in range(1, 8):
        tot = tot + red_ref[8 * t : 8 * t + 8, :]
    inv = lax.rsqrt(tot[0:3] / 4096.0 + EPS)
    coef = inv * inv * inv * (tot[3:6] / 4096.0)
    cols = []
    for x in (inv, coef):
        parts = [jnp.broadcast_to(x[t : t + 1], (D, D)).T for t in range(3)]
        cols.append(jnp.concatenate(parts, axis=0))
    r, c = cols
    i = rows_iota().astype(F32)
    inside = i < con_ref[4:5, :]
    first, last = con_ref[6:7, :], con_ref[7:8, :]
    for h in range(NH):
        rate = con_ref[h : h + 1, :]
        rog = r * og_ref[:, head(h)]
        o = o_ref[:, head(h)]
        do = rog * con_ref[8 + h : 9 + h, :] - c * o
        do_ref[:, head(h)] = do
        e = jnp.where(inside, jnp.exp(-rate * i), 0.0)
        v = dot3(split(q_ref[:, head(h)] * e), split(do), 0, 0)
        part = jnp.sum(rog * o, axis=0, keepdims=True)
        put_state(out_ref, h, v, notes(first, last, rate, part))


def k_pgrad(bnd_ref, rate_ref, q_ref, k_ref, v_ref, do_ref, c_ref, dq_ref, dk_ref):
    h = pl.program_id(0)
    rate = rate_ref[h]
    bounds = [bnd_ref[t] for t in range(5)]
    qs, ks, vs, ds = [split(x[...]) for x in (q_ref, k_ref, v_ref, do_ref)]
    cs = split(c_ref[...])
    for rb in range(3):
        n = (rb + 1) * D
        rows = slice(rb * D, n)
        dr = [x[rows] for x in ds]
        p = split(dot3(dr, [x[:n] for x in vs], 1, 1) * weights(rate, bounds, rb))
        i = rows_iota(D) + rb * D
        a = jnp.where(i < bnd_ref[5], jnp.exp(-rate * (i + 1).astype(F32)), 0.0)
        dq = dot3(p, [x[:n] for x in ks], 1, 0) + a * dot3(dr, cs, 1, 1)
        dq_ref[rows, :] = dq.astype(BF16)
        part = dot3(p, [x[rows] for x in qs], 0, 0)
        if rb == 0:
            dk_ref[0:n, :] = part
        else:
            dk_ref[0 : n - D, :] += part[: n - D]
            dk_ref[rows, :] = part[n - D :]


def k_vgrad(bnd_ref, rate_ref, q_ref, k_ref, do_ref, dv_ref):
    h = pl.program_id(0)
    rate = rate_ref[h]
    bounds = [bnd_ref[t] for t in range(5)]
    qs, ks, ds = [split(x[...]) for x in (q_ref, k_ref, do_ref)]
    for rb in range(3):
        n = (rb + 1) * D
        rows = slice(rb * D, n)
        s = dot3([x[rows] for x in qs], [x[:n] for x in ks], 1, 1)
        a = split(s * weights(rate, bounds, rb))
        part = dot3(a, [x[rows] for x in ds], 0, 0)
        if rb == 0:
            dv_ref[0:n, :] = part
        else:
            dv_ref[0 : n - D, :] += part[: n - D]
            dv_ref[rows, :] = part[n - D :]


def k_final(
    con_ref, k_ref, v_ref, st_ref, dkl_ref, dvl_ref, dk_hbm, dv_hbm, gg_ref, dk_ref, dv_ref, sems
):
    stores = []
    i = rows_iota().astype(F32)
    inside = i >= con_ref[5:6, :]
    back = float(L) - i
    for h in range(NH):
        c = jnp.where(inside, jnp.exp(-con_ref[h : h + 1, :] * back), 0.0)
        bases = [(h * PER + t) * PR for t in range(PER)]
        ss = split(jnp.concatenate([st_ref[b : b + CH, :] for b in bases], axis=0))
        gg_ref[head(h)] = st_ref[bases[0] + CH + 3, :]
        dk = dkl_ref[:, head(h)] + c * dot3(split(v_ref[:, head(h)]), ss, 1, 1)
        dv = dvl_ref[:, head(h)] + c * dot3(split(k_ref[:, head(h)]), ss, 1, 0)
        for t, (x, buf, out) in enumerate(((dk, dk_ref, dk_hbm), (dv, dv_ref, dv_hbm))):
            buf[:, head(h)] = x.astype(BF16)
            stores.append(
                pltpu.make_async_copy(
                    buf.at[:, head(h)], out.at[:, head(h)], sems.at[2 * h + t]
                )
            )
            stores[-1].start()
    for copy in stores:
        copy.wait()


def head_block():
    return pl.BlockSpec((L, D), lambda h: (0, h))


def rows_block(n):
    return pl.BlockSpec((n, D), lambda h: (h, 0))


def whole(*shape):
    return pl.BlockSpec(shape, lambda h: (0,) * len(shape))


def scalars():
    return pl.BlockSpec(memory_space=SMEM)


def sds(shape, dtype=F32):
    return jax.ShapeDtypeStruct(shape, dtype)


def far(*arrays):
    return [pltpu.with_memory_space_constraint(x, pltpu.HBM) for x in arrays]


def near(*arrays):
    return [pltpu.with_memory_space_constraint(x, pltpu.VMEM) for x in arrays]


def idle():
    return pl.BlockSpec(memory_space=pl.ANY)


def heads_call(kernel, in_specs, out_specs, out_shape, flops, scratch=(), name=None):
    return pl.pallas_call(
        kernel,
        grid=(NH,),
        in_specs=in_specs,
        out_specs=out_specs,
        out_shape=out_shape,
        scratch_shapes=list(scratch),
        compiler_params=pltpu.CompilerParams(
            dimension_semantics=("arbitrary",), vmem_limit_bytes=VMEM
        ),
        cost_estimate=pl.CostEstimate(flops=flops, transcendentals=0, bytes_accessed=3 << 20),
        name=name,
    )


def near_block():
    return pl.BlockSpec(memory_space=pltpu.VMEM)


def one_call(kernel, in_specs, out_specs, out_shape, name, flops=1 << 20, scratch=()):
    return pl.pallas_call(
        kernel,
        in_specs=in_specs,
        out_specs=out_specs,
        out_shape=out_shape,
        scratch_shapes=list(scratch),
        compiler_params=pltpu.CompilerParams(vmem_limit_bytes=VMEM),
        cost_estimate=pl.CostEstimate(flops=flops, transcendentals=0, bytes_accessed=1 << 19),
        name=name,
    )


def small_call(kernel, n_in, n_idle, out_shape, name):
    vm = near_block()
    return one_call(kernel, [vm] * n_in + [idle()] * n_idle, vm, out_shape, name)


def exchange(x, axis="seq", groups=GROUPS):
    return lax.all_to_all(x, axis, 0, 0, tiled=True, axis_index_groups=groups)


def scan_groups(payload, reverse, first=(), second=()):
    recv = exchange(payload)
    total = small_call(
        functools.partial(k_total, reverse=reverse), 1, len(first), sds((NG * PR, D)), "total"
    )(recv, *first)
    totals = exchange(total, "seq", COLUMNS)
    rows = PR if reverse else CH
    back = small_call(
        functools.partial(k_carry, reverse=reverse), 2, len(second), sds((G * rows, D)), "carry"
    )(recv, totals, *second)
    return exchange(back)


def body(queries, key_vectors, value_vectors, out_grad, norm_gain, decay_rates, segment_ids):
    hb, sc = head_block(), scalars()
    big = 9 * 2 * L * L * D * NH
    flat = pltpu.VMEM((L, NH * D), F32)
    q, k, v, rates, segs = far(queries, key_vectors, value_vectors, decay_rates, segment_ids)
    vm, work = near_block(), idle()
    payload = one_call(
        k_state,
        [work] * 4,
        vm,
        sds((G * PR, D)),
        "state",
        big // 6,
        [pltpu.VMEM((L, NH * D), F32)] * 2
        + [SMEM((L,), jnp.int32), SMEM((NH,), F32), pltpu.SemaphoreType.DMA((2 * NH + 2,))],
    )(segs, rates, k, v)
    local_out, bnd, con = heads_call(
        k_local,
        [sc, sc, hb, hb, hb, whole(NH * D)],
        [hb, sc, whole(16, D)],
        [flat, pltpu.HBM((8,), jnp.int32), pltpu.VMEM((16, D), F32)],
        big,
        name="local",
    )(segs, rates, q, k, v, *far(norm_gain))
    (bnd,) = far(bnd)
    (con,) = near(con)
    carry = scan_groups(payload, False)
    out, red = one_call(
        k_norm, [vm] * 5, [vm, vm], [flat, sds((64, D))], "norm", big // 6
    )(con, queries, carry, *near(local_out), out_grad)
    sums = exchange(red, "head", None)
    grad_out, payload = one_call(
        k_grad,
        [vm] * 5,
        [vm, vm],
        [flat, sds((G * PR, D))],
        "grad",
        big // 6,
    )(con, sums, out_grad, *near(out), queries)
    (grad_out,) = near(grad_out)
    dq, dk_local = heads_call(
        k_pgrad,
        [sc, sc, hb, hb, hb, hb, rows_block(D)],
        [hb, hb],
        [pltpu.HBM((L, NH * D), BF16), flat],
        big,
        name="pgrad",
    )(bnd, rates, q, k, v, grad_out, carry)
    dv_local = heads_call(
        k_vgrad, [sc, sc, hb, hb, hb], hb, flat, big // 2, name="vgrad"
    )(bnd, rates, q, k, *far(grad_out))
    back = scan_groups(payload, True, (dk_local,))
    dk, dv, gain_grad = one_call(
        k_final,
        [vm] * 6,
        [work, work, vm],
        [pltpu.HBM((L, NH * D), BF16)] * 2 + [sds((NH * D,))],
        "final",
        big // 6,
        [pltpu.VMEM((L, NH * D), BF16)] * 2 + [pltpu.SemaphoreType.DMA((2 * NH,))],
    )(con, key_vectors, value_vectors, back, *near(dk_local, dv_local))
    return dq, dk, dv, gain_grad


def solution(mesh):
    return jax.shard_map(
        body,
        mesh=mesh,
        in_specs=(
            P("seq", "head"),
            P("seq", "head"),
            P("seq", "head"),
            P("seq", "head"),
            P("head"),
            P("head"),
            P("seq"),
        ),
        out_specs=(P("seq", "head"), P("seq", "head"), P("seq", "head"), P("head")),
        check_vma=False,
    )
```

```python
import functools
import jax
import jax.numpy as jnp
from jax import lax
from jax.experimental import pallas as pl
from jax.experimental.pallas import tpu as pltpu
from jax.sharding import PartitionSpec as P

F32 = jnp.float32
BF16 = jnp.bfloat16
D = 128
L = 384
NH = 4
G = 16
NG = 4
PER = 4
CH = 32
PR = CH + 8
EPS = 1e-06
GROUPS = [[G * z + i for i in range(G)] for z in range(NG)]
COLUMNS = [[G * z + i for z in range(NG)] for i in range(G)]
SMEM = pltpu.SMEM
VMEM = 12 << 20


def split(x):
    hi = x.astype(BF16)
    return hi, (x - hi.astype(F32)).astype(BF16)


def dot3(a, b, ca, cb):
    dims = (((ca,), (cb,)), ((), ()))
    dg = functools.partial(lax.dot_general, dimension_numbers=dims, preferred_element_type=F32)
    return dg(a[0], b[0]) + (dg(a[0], b[1]) + dg(a[1], b[0]))


def first_at_least(seg_ref, value):
    lo = jnp.int32(0)
    size = jnp.int32(0)
    for step in (256, 128, 64, 32, 16, 8, 4, 2, 1):
        probe = lo + step
        inside = probe <= L
        below = seg_ref[jnp.minimum(probe, L) - 1] < value
        lo = jnp.where(inside & below, probe, lo)
    return lo + size


def rows_iota(n=L):
    return lax.broadcasted_iota(jnp.int32, (n, D), 0)


def seg_of(places, bounds):
    s = jnp.zeros(places.shape, jnp.int32)
    for b in bounds:
        s = s + (places >= b).astype(jnp.int32)
    return s


GAIN = 3


def notes(first, last, rate, gains=()):
    row = lax.broadcasted_iota(jnp.int32, (8, D), 0)
    tile = jnp.where(row == 0, first, jnp.where(row == 1, last, jnp.where(row == 2, rate, 0.0)))
    for t, gain in enumerate(gains):
        tile = jnp.where(row == GAIN + t, gain, tile)
    return tile


def put_state(out_ref, h, state):
    for t in range(PER):
        base = (h * PER + t) * PR
        out_ref[base : base + CH, :] = state[t * CH : (t + 1) * CH]


def put_note(out_ref, h, note):
    for t in range(PER):
        base = (h * PER + t) * PR
        out_ref[base + CH : base + PR, :] = note


def head(h):
    return slice(h * D, (h + 1) * D)


def k_state(seg_hbm, rate_hbm, k_hbm, v_hbm, out_ref, k_ref, v_ref, seg_ref, rate_ref, sems):
    small = [
        pltpu.make_async_copy(seg_hbm, seg_ref, sems.at[2 * NH]),
        pltpu.make_async_copy(rate_hbm, rate_ref, sems.at[2 * NH + 1]),
    ]
    for copy in small:
        copy.start()
    copies = []
    for h in range(NH):
        for t, (src, dst) in enumerate(((k_hbm, k_ref), (v_hbm, v_ref))):
            copies.append(
                pltpu.make_async_copy(src.at[:, head(h)], dst.at[:, head(h)], sems.at[2 * h + t])
            )
            copies[-1].start()
    for copy in small:
        copy.wait()
    first, last = seg_ref[0], seg_ref[L - 1]
    start = first_at_least(seg_ref, last)
    i = rows_iota()
    back = (L - 1 - i).astype(F32)
    for h in range(NH):
        rate = rate_ref[h]
        b = jnp.where(i >= start, jnp.exp(-rate * back), 0.0)
        copies[2 * h].wait()
        copies[2 * h + 1].wait()
        u = dot3(split(k_ref[:, head(h)] * b), split(v_ref[:, head(h)]), 0, 0)
        put_state(out_ref, h, u)
        put_note(out_ref, h, notes(first.astype(F32), last.astype(F32), rate))


def weights(rate, bounds, rb):
    n = (rb + 1) * D
    i = lax.broadcasted_iota(jnp.int32, (D, n), 0) + rb * D
    j = lax.broadcasted_iota(jnp.int32, (D, n), 1)
    si = seg_of(lax.broadcasted_iota(jnp.int32, (D, 1), 0) + rb * D, bounds)
    sj = seg_of(lax.broadcasted_iota(jnp.int32, (1, n), 1), bounds)
    dist = jnp.maximum(i - j, 0).astype(F32)
    return jnp.where((i >= j) & (si == sj), jnp.exp(-rate * dist), 0.0)


def k_local(seg_ref, rate_ref, q_ref, k_ref, v_ref, gain_ref, o_ref, bnd_ref, con_ref):
    h = pl.program_id(0)

    @pl.when(h == 0)
    def _():
        for t in range(1, 6):
            bnd_ref[t - 1] = first_at_least(seg_ref, t)
        bnd_ref[5] = first_at_least(seg_ref, seg_ref[0] + 1)
        bnd_ref[6] = first_at_least(seg_ref, seg_ref[L - 1])
        bnd_ref[7] = 0
        row = lax.broadcasted_iota(jnp.int32, (8, D), 0)
        tile = jnp.zeros((8, D), F32)
        values = [rate_ref[t] for t in range(NH)]
        values += [bnd_ref[5], bnd_ref[6], seg_ref[0], seg_ref[L - 1]]
        for t, value in enumerate(values):
            tile = jnp.where(row == t, value.astype(F32), tile)
        con_ref[0:8, :] = tile
        for t in range(NH):
            con_ref[8 + t : 9 + t, :] = gain_ref[head(t)].reshape(1, D)
        con_ref[12:16, :] = jnp.zeros((4, D), F32)

    bounds = [bnd_ref[t] for t in range(5)]
    rate = rate_ref[h]
    qs, ks, vs = split(q_ref[...]), split(k_ref[...]), split(v_ref[...])
    for rb in range(3):
        n = (rb + 1) * D
        qr = [x[rb * D : n] for x in qs]
        kc = [x[:n] for x in ks]
        vc = [x[:n] for x in vs]
        a = dot3(qr, kc, 1, 1) * weights(rate, bounds, rb)
        o_ref[rb * D : n, :] = dot3(split(a), vc, 1, 0)


def chain(recv_ref, state, reverse, take):
    rate = recv_ref[CH + 2 : CH + 3, :]
    lam = jnp.exp(-rate * float(L))
    order = range(G - 1, -1, -1) if reverse else range(G)
    prev = None
    for i in order:
        base = i * PR
        enter = recv_ref[base + CH + (1 if reverse else 0) : base + CH + (2 if reverse else 1), :]
        leave = recv_ref[base + CH + (0 if reverse else 1) : base + CH + (1 if reverse else 2), :]
        if prev is not None:
            state = jnp.where(prev == enter, 1.0, 0.0) * state
        take(i, state)
        here = recv_ref[base : base + CH, :]
        if state is None:
            state = here
        else:
            state = here + jnp.where(enter == leave, lam, 0.0) * state
        prev = leave
    return state


def k_total(recv_ref, *rest, reverse):
    t_ref = rest[-1]
    t_ref[0:CH, :] = chain(recv_ref, jnp.zeros((CH, D), F32), reverse, lambda i, s: None)
    note = recv_ref[CH:PR, :]
    row = lax.broadcasted_iota(jnp.int32, (8, D), 0)
    out = jnp.where(row == 1, recv_ref[(G - 1) * PR + CH : G * PR, :], note)
    if reverse:
        for i in range(1, G):
            note = note + recv_ref[i * PR + CH : (i + 1) * PR, :]
        out = jnp.where(row >= GAIN, note, out)
    t_ref[CH:PR, :] = out
    for t in range(1, NG):
        t_ref[t * PR : (t + 1) * PR, :] = t_ref[0:PR, :]


def k_carry(recv_ref, t_ref, out_ref, *rest, reverse):
    mine = lax.div(lax.axis_index("seq"), G)
    rate = recv_ref[CH + 2 : CH + 3, :]
    edge = G - 1 if reverse else 0
    row = edge * PR + CH + (1 if reverse else 0)
    enter = recv_ref[row : row + 1, :]
    state = jnp.zeros((CH, D), F32)
    gain = jnp.zeros((8, D), F32)
    for g in range(NG):
        base = g * PR
        leave = base + CH + (0 if reverse else 1)
        gap = (g - 1 - mine) if reverse else (mine - 1 - g)
        same = (t_ref[leave : leave + 1, :] == enter) & (gap >= 0)
        power = jnp.maximum(gap, 0).astype(F32) * float(L * G)
        state = state + jnp.where(same, jnp.exp(-rate * power), 0.0) * t_ref[base : base + CH, :]
        gain = gain + t_ref[base + CH : base + PR, :]
    if reverse:
        rest[0][...] = gain

    def take(i, s):
        out_ref[i * CH : (i + 1) * CH, :] = s

    chain(recv_ref, state, reverse, take)


def k_norm(con_ref, q_ref, c_ref, ol_ref, og_ref, o_ref, red_ref):
    i = rows_iota().astype(F32)
    ahead = i + 1.0
    inside = i < con_ref[4:5, :]
    sq = pr = None
    for h in range(NH):
        a = jnp.where(inside, jnp.exp(-con_ref[h : h + 1, :] * ahead), 0.0)
        o = ol_ref[:, head(h)] + a * dot3(split(q_ref[:, head(h)]), split(c_ref[head(h), :]), 1, 0)
        o_ref[:, head(h)] = o
        g = og_ref[:, head(h)] * con_ref[8 + h : 9 + h, :]
        sq = o * o if h == 0 else sq + o * o
        pr = g * o if h == 0 else pr + g * o
    ones = jnp.ones((8, D), BF16)
    dims = (((1,), (1,)), ((), ()))
    dg = functools.partial(lax.dot_general, dimension_numbers=dims, preferred_element_type=F32)
    rows = []
    for x in (sq, pr):
        hi, lo = split(x)
        both = dg(ones, hi) + dg(ones, lo)
        rows += [both[0:1, head(t)] for t in range(3)]
    tile = jnp.concatenate(rows + [jnp.zeros((2, D), F32)], axis=0)
    for t in range(8):
        red_ref[8 * t : 8 * t + 8, :] = tile


def k_grad(
    con_ref, red_ref, og_ref, o_ref, q_ref, do_ref, out_ref
):
    tot = red_ref[0:8, :]
    for t in range(1, 8):
        tot = tot + red_ref[8 * t : 8 * t + 8, :]
    inv = lax.rsqrt(tot[0:3] / 4096.0 + EPS)
    coef = inv * inv * inv * (tot[3:6] / 4096.0)
    cols = []
    for x in (inv, coef):
        parts = [jnp.broadcast_to(x[t : t + 1], (D, D)).T for t in range(3)]
        cols.append(jnp.concatenate(parts, axis=0))
    r, c = cols
    i = rows_iota().astype(F32)
    inside = i < con_ref[4:5, :]
    first, last = con_ref[6:7, :], con_ref[7:8, :]
    gains = []
    for h in range(NH):
        rate = con_ref[h : h + 1, :]
        rog = r * og_ref[:, head(h)]
        o = o_ref[:, head(h)]
        do = rog * con_ref[8 + h : 9 + h, :] - c * o
        do_ref[:, head(h)] = do
        e = jnp.where(inside, jnp.exp(-rate * i), 0.0)
        v = dot3(split(q_ref[:, head(h)] * e), split(do), 0, 0)
        gains.append(jnp.sum(rog * o, axis=0, keepdims=True))
        put_state(out_ref, h, v)
    for h in range(NH):
        put_note(out_ref, h, notes(first, last, con_ref[h : h + 1, :], gains))


def k_pgrad(bnd_ref, rate_ref, q_ref, k_ref, v_ref, do_ref, c_ref, dq_ref, dk_ref):
    h = pl.program_id(0)
    rate = rate_ref[h]
    bounds = [bnd_ref[t] for t in range(5)]
    qs, ks, vs, ds = [split(x[...]) for x in (q_ref, k_ref, v_ref, do_ref)]
    cs = split(c_ref[...])
    for rb in range(3):
        n = (rb + 1) * D
        rows = slice(rb * D, n)
        dr = [x[rows] for x in ds]
        p = split(dot3(dr, [x[:n] for x in vs], 1, 1) * weights(rate, bounds, rb))
        i = rows_iota(D) + rb * D
        a = jnp.where(i < bnd_ref[5], jnp.exp(-rate * (i + 1).astype(F32)), 0.0)
        dq = dot3(p, [x[:n] for x in ks], 1, 0) + a * dot3(dr, cs, 1, 1)
        dq_ref[rows, :] = dq.astype(BF16)
        part = dot3(p, [x[rows] for x in qs], 0, 0)
        if rb == 0:
            dk_ref[0:n, :] = part
        else:
            dk_ref[0 : n - D, :] += part[: n - D]
            dk_ref[rows, :] = part[n - D :]


def k_vgrad(bnd_ref, rate_ref, q_ref, k_ref, do_ref, dv_ref):
    h = pl.program_id(0)
    rate = rate_ref[h]
    bounds = [bnd_ref[t] for t in range(5)]
    qs, ks, ds = [split(x[...]) for x in (q_ref, k_ref, do_ref)]
    for rb in range(3):
        n = (rb + 1) * D
        rows = slice(rb * D, n)
        s = dot3([x[rows] for x in qs], [x[:n] for x in ks], 1, 1)
        a = split(s * weights(rate, bounds, rb))
        part = dot3(a, [x[rows] for x in ds], 0, 0)
        if rb == 0:
            dv_ref[0:n, :] = part
        else:
            dv_ref[0 : n - D, :] += part[: n - D]
            dv_ref[rows, :] = part[n - D :]


def k_final(
    con_ref, k_ref, v_ref, st_ref, dkl_ref, dvl_ref, gain_ref,
    dk_hbm, dv_hbm, gg_ref, dk_ref, dv_ref, sems,
):
    stores = []
    i = rows_iota().astype(F32)
    inside = i >= con_ref[5:6, :]
    back = float(L) - i
    for h in range(NH):
        c = jnp.where(inside, jnp.exp(-con_ref[h : h + 1, :] * back), 0.0)
        ss = split(st_ref[head(h), :])
        gg_ref[head(h)] = gain_ref[GAIN + h, :]
        dk = dkl_ref[:, head(h)] + c * dot3(split(v_ref[:, head(h)]), ss, 1, 1)
        dv = dvl_ref[:, head(h)] + c * dot3(split(k_ref[:, head(h)]), ss, 1, 0)
        for t, (x, buf, out) in enumerate(((dk, dk_ref, dk_hbm), (dv, dv_ref, dv_hbm))):
            buf[:, head(h)] = x.astype(BF16)
            stores.append(
                pltpu.make_async_copy(
                    buf.at[:, head(h)], out.at[:, head(h)], sems.at[2 * h + t]
                )
            )
            stores[-1].start()
    for copy in stores:
        copy.wait()


def head_block():
    return pl.BlockSpec((L, D), lambda h: (0, h))


def rows_block(n):
    return pl.BlockSpec((n, D), lambda h: (h, 0))


def whole(*shape):
    return pl.BlockSpec(shape, lambda h: (0,) * len(shape))


def scalars():
    return pl.BlockSpec(memory_space=SMEM)


def sds(shape, dtype=F32):
    return jax.ShapeDtypeStruct(shape, dtype)


def far(*arrays):
    return [pltpu.with_memory_space_constraint(x, pltpu.HBM) for x in arrays]


def near(*arrays):
    return [pltpu.with_memory_space_constraint(x, pltpu.VMEM) for x in arrays]


def idle():
    return pl.BlockSpec(memory_space=pl.ANY)


def heads_call(kernel, in_specs, out_specs, out_shape, flops, scratch=(), name=None):
    return pl.pallas_call(
        kernel,
        grid=(NH,),
        in_specs=in_specs,
        out_specs=out_specs,
        out_shape=out_shape,
        scratch_shapes=list(scratch),
        compiler_params=pltpu.CompilerParams(
            dimension_semantics=("arbitrary",), vmem_limit_bytes=VMEM
        ),
        cost_estimate=pl.CostEstimate(flops=flops, transcendentals=0, bytes_accessed=3 << 20),
        name=name,
    )


def near_block():
    return pl.BlockSpec(memory_space=pltpu.VMEM)


def one_call(kernel, in_specs, out_specs, out_shape, name, flops=1 << 20, scratch=()):
    return pl.pallas_call(
        kernel,
        in_specs=in_specs,
        out_specs=out_specs,
        out_shape=out_shape,
        scratch_shapes=list(scratch),
        compiler_params=pltpu.CompilerParams(vmem_limit_bytes=VMEM),
        cost_estimate=pl.CostEstimate(flops=flops, transcendentals=0, bytes_accessed=1 << 19),
        name=name,
    )


def small_call(kernel, n_in, n_idle, out_shape, name):
    vm = near_block()
    return one_call(kernel, [vm] * n_in + [idle()] * n_idle, vm, out_shape, name)


def exchange(x, axis="seq", groups=GROUPS):
    return lax.all_to_all(x, axis, 0, 0, tiled=True, axis_index_groups=groups)


def scan_groups(payload, reverse, order=()):
    vm = near_block()
    recv = exchange(payload)
    total = small_call(
        functools.partial(k_total, reverse=reverse), 1, len(order), sds((NG * PR, D)), "total"
    )(recv, *order)
    totals = exchange(total, "seq", COLUMNS)
    shapes = [sds((G * CH, D))] + ([pltpu.VMEM((8, D), F32)] if reverse else [])
    back, *gain = one_call(
        functools.partial(k_carry, reverse=reverse), [vm] * 2, [vm] * len(shapes), shapes, "carry"
    )(recv, totals)
    return exchange(back), *near(*gain)


def body(queries, key_vectors, value_vectors, out_grad, norm_gain, decay_rates, segment_ids):
    hb, sc = head_block(), scalars()
    big = 9 * 2 * L * L * D * NH
    flat = pltpu.VMEM((L, NH * D), F32)
    q, k, v, rates, segs = far(queries, key_vectors, value_vectors, decay_rates, segment_ids)
    vm, work = near_block(), idle()
    payload = one_call(
        k_state,
        [work] * 4,
        vm,
        sds((G * PR, D)),
        "state",
        big // 6,
        [pltpu.VMEM((L, NH * D), F32)] * 2
        + [SMEM((L,), jnp.int32), SMEM((NH,), F32), pltpu.SemaphoreType.DMA((2 * NH + 2,))],
    )(segs, rates, k, v)
    local_out, bnd, con = heads_call(
        k_local,
        [sc, sc, hb, hb, hb, whole(NH * D)],
        [hb, sc, whole(16, D)],
        [flat, pltpu.HBM((8,), jnp.int32), pltpu.VMEM((16, D), F32)],
        big,
        name="local",
    )(segs, rates, q, k, v, *far(norm_gain))
    (bnd,) = far(bnd)
    (con,) = near(con)
    (carry,) = scan_groups(payload, False)
    out, red = one_call(
        k_norm, [vm] * 5, [vm, vm], [flat, sds((64, D))], "norm", big // 6
    )(con, queries, carry, *near(local_out), out_grad)
    sums = exchange(red, "head", None)
    grad_out, payload = one_call(
        k_grad,
        [vm] * 5,
        [vm, vm],
        [flat, sds((G * PR, D))],
        "grad",
        big // 6,
    )(con, sums, out_grad, *near(out), queries)
    (grad_out,) = near(grad_out)
    dq, dk_local = heads_call(
        k_pgrad,
        [sc, sc, hb, hb, hb, hb, rows_block(D)],
        [hb, hb],
        [pltpu.HBM((L, NH * D), BF16), flat],
        big,
        name="pgrad",
    )(bnd, rates, q, k, v, grad_out, carry)
    dv_local = heads_call(
        k_vgrad, [sc, sc, hb, hb, hb], hb, flat, big // 2, name="vgrad"
    )(bnd, rates, q, k, *far(grad_out))
    back, gain = scan_groups(payload, True, (dk_local,))
    dk, dv, gain_grad = one_call(
        k_final,
        [vm] * 7,
        [work, work, vm],
        [pltpu.HBM((L, NH * D), BF16)] * 2 + [sds((NH * D,))],
        "final",
        big // 6,
        [pltpu.VMEM((L, NH * D), BF16)] * 2 + [pltpu.SemaphoreType.DMA((2 * NH,))],
    )(con, key_vectors, value_vectors, back, *near(dk_local, dv_local), gain)
    return dq, dk, dv, gain_grad


def solution(mesh):
    return jax.shard_map(
        body,
        mesh=mesh,
        in_specs=(
            P("seq", "head"),
            P("seq", "head"),
            P("seq", "head"),
            P("seq", "head"),
            P("head"),
            P("head"),
            P("seq"),
        ),
        out_specs=(P("seq", "head"), P("seq", "head"), P("seq", "head"), P("head")),
        check_vma=False,
    )
```

```python
import functools
import jax
import jax.numpy as jnp
from jax import lax
from jax.experimental import pallas as pl
from jax.experimental.pallas import tpu as pltpu
from jax.sharding import PartitionSpec as P

F32 = jnp.float32
BF16 = jnp.bfloat16
D = 128
L = 384
NH = 4
G = 16
NG = 4
PER = 4
CH = 32
PR = CH + 8
EPS = 1e-06
GROUPS = [[G * z + i for i in range(G)] for z in range(NG)]
COLUMNS = [[G * z + i for z in range(NG)] for i in range(G)]
SMEM = pltpu.SMEM
VMEM = 12 << 20


def split(x):
    hi = x.astype(BF16)
    return hi, (x - hi.astype(F32)).astype(BF16)


def dot3(a, b, ca, cb):
    dims = (((ca,), (cb,)), ((), ()))
    dg = functools.partial(lax.dot_general, dimension_numbers=dims, preferred_element_type=F32)
    return dg(a[0], b[0]) + (dg(a[0], b[1]) + dg(a[1], b[0]))


def first_at_least(seg_ref, value):
    lo = jnp.int32(0)
    size = jnp.int32(0)
    for step in (256, 128, 64, 32, 16, 8, 4, 2, 1):
        probe = lo + step
        inside = probe <= L
        below = seg_ref[jnp.minimum(probe, L) - 1] < value
        lo = jnp.where(inside & below, probe, lo)
    return lo + size


def rows_iota(n=L):
    return lax.broadcasted_iota(jnp.int32, (n, D), 0)


def seg_of(places, bounds):
    s = jnp.zeros(places.shape, jnp.int32)
    for b in bounds:
        s = s + (places >= b).astype(jnp.int32)
    return s


GAIN = 3


def notes(first, last, rate, gains=()):
    row = lax.broadcasted_iota(jnp.int32, (8, D), 0)
    tile = jnp.where(row == 0, first, jnp.where(row == 1, last, jnp.where(row == 2, rate, 0.0)))
    for t, gain in enumerate(gains):
        tile = jnp.where(row == GAIN + t, gain, tile)
    return tile


def put_state(out_ref, h, state):
    for t in range(PER):
        base = (h * PER + t) * PR
        out_ref[base : base + CH, :] = state[t * CH : (t + 1) * CH]


def put_note(out_ref, h, note):
    for t in range(PER):
        base = (h * PER + t) * PR
        out_ref[base + CH : base + PR, :] = note


def head(h):
    return slice(h * D, (h + 1) * D)


def k_state(seg_hbm, rate_hbm, k_hbm, v_hbm, out_ref, k_ref, v_ref, seg_ref, rate_ref, sems):
    small = [
        pltpu.make_async_copy(seg_hbm, seg_ref, sems.at[2 * NH]),
        pltpu.make_async_copy(rate_hbm, rate_ref, sems.at[2 * NH + 1]),
    ]
    for copy in small:
        copy.start()
    copies = []
    for h in range(NH):
        for t, (src, dst) in enumerate(((k_hbm, k_ref), (v_hbm, v_ref))):
            copies.append(
                pltpu.make_async_copy(src.at[:, head(h)], dst.at[:, head(h)], sems.at[2 * h + t])
            )
            copies[-1].start()
    for copy in small:
        copy.wait()
    first, last = seg_ref[0], seg_ref[L - 1]
    start = first_at_least(seg_ref, last)
    i = rows_iota()
    back = (L - 1 - i).astype(F32)
    for h in range(NH):
        rate = rate_ref[h]
        b = jnp.where(i >= start, jnp.exp(-rate * back), 0.0)
        copies[2 * h].wait()
        copies[2 * h + 1].wait()
        u = dot3(split(k_ref[:, head(h)] * b), split(v_ref[:, head(h)]), 0, 0)
        put_state(out_ref, h, u)
        put_note(out_ref, h, notes(first.astype(F32), last.astype(F32), rate))


def weights(rate, bounds, rb):
    n = (rb + 1) * D
    i = lax.broadcasted_iota(jnp.int32, (D, n), 0) + rb * D
    j = lax.broadcasted_iota(jnp.int32, (D, n), 1)
    si = seg_of(lax.broadcasted_iota(jnp.int32, (D, 1), 0) + rb * D, bounds)
    sj = seg_of(lax.broadcasted_iota(jnp.int32, (1, n), 1), bounds)
    dist = jnp.maximum(i - j, 0).astype(F32)
    return jnp.where((i >= j) & (si == sj), jnp.exp(-rate * dist), 0.0)


def k_local(seg_ref, rate_ref, q_ref, k_ref, v_ref, gain_ref, o_ref, bnd_ref, con_ref):
    h = pl.program_id(0)

    @pl.when(h == 0)
    def _():
        for t in range(1, 6):
            bnd_ref[t - 1] = first_at_least(seg_ref, t)
        bnd_ref[5] = first_at_least(seg_ref, seg_ref[0] + 1)
        bnd_ref[6] = first_at_least(seg_ref, seg_ref[L - 1])
        bnd_ref[7] = 0
        row = lax.broadcasted_iota(jnp.int32, (8, D), 0)
        tile = jnp.zeros((8, D), F32)
        values = [rate_ref[t] for t in range(NH)]
        values += [bnd_ref[5], bnd_ref[6], seg_ref[0], seg_ref[L - 1]]
        for t, value in enumerate(values):
            tile = jnp.where(row == t, value.astype(F32), tile)
        con_ref[0:8, :] = tile
        for t in range(NH):
            con_ref[8 + t : 9 + t, :] = gain_ref[head(t)].reshape(1, D)
        con_ref[12:16, :] = jnp.zeros((4, D), F32)

    bounds = [bnd_ref[t] for t in range(5)]
    rate = rate_ref[h]
    qs, ks, vs = split(q_ref[...]), split(k_ref[...]), split(v_ref[...])
    for rb in range(3):
        n = (rb + 1) * D
        qr = [x[rb * D : n] for x in qs]
        kc = [x[:n] for x in ks]
        vc = [x[:n] for x in vs]
        a = dot3(qr, kc, 1, 1) * weights(rate, bounds, rb)
        o_ref[rb * D : n, :] = dot3(split(a), vc, 1, 0)


def chain(recv_ref, state, reverse, take):
    rate = recv_ref[CH + 2 : CH + 3, :]
    lam = jnp.exp(-rate * float(L))
    order = range(G - 1, -1, -1) if reverse else range(G)
    prev = None
    for i in order:
        base = i * PR
        enter = recv_ref[base + CH + (1 if reverse else 0) : base + CH + (2 if reverse else 1), :]
        leave = recv_ref[base + CH + (0 if reverse else 1) : base + CH + (1 if reverse else 2), :]
        if prev is not None:
            state = jnp.where(prev == enter, 1.0, 0.0) * state
        take(i, state)
        here = recv_ref[base : base + CH, :]
        if state is None:
            state = here
        else:
            state = here + jnp.where(enter == leave, lam, 0.0) * state
        prev = leave
    return state


def k_total(recv_ref, *rest, reverse):
    t_ref = rest[-1]
    t_ref[0:CH, :] = chain(recv_ref, jnp.zeros((CH, D), F32), reverse, lambda i, s: None)
    note = recv_ref[CH:PR, :]
    row = lax.broadcasted_iota(jnp.int32, (8, D), 0)
    out = jnp.where(row == 1, recv_ref[(G - 1) * PR + CH : G * PR, :], note)
    if reverse:
        for i in range(1, G):
            note = note + recv_ref[i * PR + CH : (i + 1) * PR, :]
        out = jnp.where(row >= GAIN, note, out)
    t_ref[CH:PR, :] = out
    for t in range(1, NG):
        t_ref[t * PR : (t + 1) * PR, :] = t_ref[0:PR, :]


def k_carry(recv_ref, t_ref, out_ref, *rest, reverse):
    mine = lax.div(lax.axis_index("seq"), G)
    rate = recv_ref[CH + 2 : CH + 3, :]
    edge = G - 1 if reverse else 0
    row = edge * PR + CH + (1 if reverse else 0)
    enter = recv_ref[row : row + 1, :]
    state = jnp.zeros((CH, D), F32)
    gain = jnp.zeros((8, D), F32)
    for g in range(NG):
        base = g * PR
        leave = base + CH + (0 if reverse else 1)
        gap = (g - 1 - mine) if reverse else (mine - 1 - g)
        same = (t_ref[leave : leave + 1, :] == enter) & (gap >= 0)
        power = jnp.maximum(gap, 0).astype(F32) * float(L * G)
        state = state + jnp.where(same, jnp.exp(-rate * power), 0.0) * t_ref[base : base + CH, :]
        gain = gain + t_ref[base + CH : base + PR, :]
    if reverse:
        rest[0][...] = gain

    def take(i, s):
        out_ref[i * CH : (i + 1) * CH, :] = s

    chain(recv_ref, state, reverse, take)


def k_norm(con_ref, q_ref, c_ref, ol_ref, og_ref, o_ref, red_ref):
    i = rows_iota().astype(F32)
    ahead = i + 1.0
    inside = i < con_ref[4:5, :]
    sq = pr = None
    for h in range(NH):
        a = jnp.where(inside, jnp.exp(-con_ref[h : h + 1, :] * ahead), 0.0)
        o = ol_ref[:, head(h)] + a * dot3(split(q_ref[:, head(h)]), split(c_ref[head(h), :]), 1, 0)
        o_ref[:, head(h)] = o
        g = og_ref[:, head(h)] * con_ref[8 + h : 9 + h, :]
        sq = o * o if h == 0 else sq + o * o
        pr = g * o if h == 0 else pr + g * o
    ones = jnp.ones((8, D), BF16)
    dims = (((1,), (1,)), ((), ()))
    dg = functools.partial(lax.dot_general, dimension_numbers=dims, preferred_element_type=F32)
    rows = []
    for x in (sq, pr):
        hi, lo = split(x)
        both = dg(ones, hi) + dg(ones, lo)
        rows += [both[0:1, head(t)] for t in range(3)]
    tile = jnp.concatenate(rows + [jnp.zeros((2, D), F32)], axis=0)
    for t in range(8):
        red_ref[8 * t : 8 * t + 8, :] = tile


def k_grad(
    con_ref, red_ref, og_ref, o_ref, q_ref, do_ref, out_ref
):
    tot = red_ref[0:8, :]
    for t in range(1, 8):
        tot = tot + red_ref[8 * t : 8 * t + 8, :]
    inv = lax.rsqrt(tot[0:3] / 4096.0 + EPS)
    coef = inv * inv * inv * (tot[3:6] / 4096.0)
    cols = []
    for x in (inv, coef):
        parts = [jnp.broadcast_to(x[t : t + 1], (D, D)).T for t in range(3)]
        cols.append(jnp.concatenate(parts, axis=0))
    r, c = cols
    i = rows_iota().astype(F32)
    inside = i < con_ref[4:5, :]
    first, last = con_ref[6:7, :], con_ref[7:8, :]
    gains = []
    for h in range(NH):
        rate = con_ref[h : h + 1, :]
        rog = r * og_ref[:, head(h)]
        o = o_ref[:, head(h)]
        do = rog * con_ref[8 + h : 9 + h, :] - c * o
        do_ref[:, head(h)] = do
        e = jnp.where(inside, jnp.exp(-rate * i), 0.0)
        v = dot3(split(q_ref[:, head(h)] * e), split(do), 0, 0)
        gains.append(jnp.sum(rog * o, axis=0, keepdims=True))
        put_state(out_ref, h, v)
    for h in range(NH):
        put_note(out_ref, h, notes(first, last, con_ref[h : h + 1, :], gains))


def dot3k(a, b, ca, cb):
    left = jnp.concatenate([a[0], a[1], a[0]], axis=ca)
    right = jnp.concatenate([b[0], b[0], b[1]], axis=cb)
    dims = (((ca,), (cb,)), ((), ()))
    return lax.dot_general(left, right, dims, preferred_element_type=F32)


def k_back(
    bnd_ref, rate_ref, q_ref, k_ref, v_ref, do_ref, c_ref, after, dq_ref, both_ref
):
    h = pl.program_id(0)
    rate = rate_ref[h]
    bounds = [bnd_ref[t] for t in range(5)]
    qs, ks, vs, ds = [split(x[...]) for x in (q_ref, k_ref, v_ref, do_ref)]
    cs = split(c_ref[...])
    for rb in range(3):
        n = (rb + 1) * D
        rows = slice(rb * D, n)
        qr, dr = [x[rows] for x in qs], [x[rows] for x in ds]
        kc, vc = [x[:n] for x in ks], [x[:n] for x in vs]
        w = weights(rate, bounds, rb)
        p = split(dot3k(dr, vc, 1, 1) * w)
        a = split(dot3k(qr, kc, 1, 1) * w)
        i = rows_iota(D) + rb * D
        coef = jnp.where(i < bnd_ref[5], jnp.exp(-rate * (i + 1).astype(F32)), 0.0)
        dq = dot3k(p, kc, 1, 0) + coef * dot3k(dr, cs, 1, 1)
        dq_ref[rows, :] = dq.astype(BF16)
        for t, part in enumerate((dot3(p, qr, 0, 0), dot3(a, dr, 0, 0))):
            if rb > 0:
                both_ref[t, 0 : n - D, :] += part[: n - D]
            both_ref[t, rows, :] = part[n - D :]


def k_final(
    con_ref, k_ref, v_ref, st_ref, both_ref, gain_ref,
    dk_hbm, dv_hbm, gg_ref, dk_ref, dv_ref, sems,
):
    stores = []
    i = rows_iota().astype(F32)
    inside = i >= con_ref[5:6, :]
    back = float(L) - i
    for h in range(NH):
        c = jnp.where(inside, jnp.exp(-con_ref[h : h + 1, :] * back), 0.0)
        ss = split(st_ref[head(h), :])
        gg_ref[head(h)] = gain_ref[GAIN + h, :]
        dk = both_ref[0, :, head(h)] + c * dot3(split(v_ref[:, head(h)]), ss, 1, 1)
        dv = both_ref[1, :, head(h)] + c * dot3(split(k_ref[:, head(h)]), ss, 1, 0)
        for t, (x, buf, out) in enumerate(((dk, dk_ref, dk_hbm), (dv, dv_ref, dv_hbm))):
            buf[:, head(h)] = x.astype(BF16)
            stores.append(
                pltpu.make_async_copy(
                    buf.at[:, head(h)], out.at[:, head(h)], sems.at[2 * h + t]
                )
            )
            stores[-1].start()
    for copy in stores:
        copy.wait()


def head_block():
    return pl.BlockSpec((L, D), lambda h: (0, h))


def rows_block(n):
    return pl.BlockSpec((n, D), lambda h: (h, 0))


def whole(*shape):
    return pl.BlockSpec(shape, lambda h: (0,) * len(shape))


def scalars():
    return pl.BlockSpec(memory_space=SMEM)


def sds(shape, dtype=F32):
    return jax.ShapeDtypeStruct(shape, dtype)


def far(*arrays):
    return [pltpu.with_memory_space_constraint(x, pltpu.HBM) for x in arrays]


def near(*arrays):
    return [pltpu.with_memory_space_constraint(x, pltpu.VMEM) for x in arrays]


def idle():
    return pl.BlockSpec(memory_space=pl.ANY)


def heads_call(kernel, in_specs, out_specs, out_shape, flops, scratch=(), name=None):
    return pl.pallas_call(
        kernel,
        grid=(NH,),
        in_specs=in_specs,
        out_specs=out_specs,
        out_shape=out_shape,
        scratch_shapes=list(scratch),
        compiler_params=pltpu.CompilerParams(
            dimension_semantics=("arbitrary",), vmem_limit_bytes=VMEM
        ),
        cost_estimate=pl.CostEstimate(flops=flops, transcendentals=0, bytes_accessed=3 << 20),
        name=name,
    )


def near_block():
    return pl.BlockSpec(memory_space=pltpu.VMEM)


def one_call(kernel, in_specs, out_specs, out_shape, name, flops=1 << 20, scratch=()):
    return pl.pallas_call(
        kernel,
        in_specs=in_specs,
        out_specs=out_specs,
        out_shape=out_shape,
        scratch_shapes=list(scratch),
        compiler_params=pltpu.CompilerParams(vmem_limit_bytes=VMEM),
        cost_estimate=pl.CostEstimate(flops=flops, transcendentals=0, bytes_accessed=1 << 19),
        name=name,
    )


def small_call(kernel, n_in, n_idle, out_shape, name):
    vm = near_block()
    return one_call(kernel, [vm] * n_in + [idle()] * n_idle, vm, out_shape, name)


def exchange(x, axis="seq", groups=GROUPS):
    return lax.all_to_all(x, axis, 0, 0, tiled=True, axis_index_groups=groups)


def scan_groups(payload, reverse):
    vm = near_block()
    recv = exchange(payload)
    total = small_call(
        functools.partial(k_total, reverse=reverse), 1, 0, sds((NG * PR, D)), "total"
    )(recv)
    totals = exchange(total, "seq", COLUMNS)
    shapes = [sds((G * CH, D))] + ([pltpu.VMEM((8, D), F32)] if reverse else [])
    back, *gain = one_call(
        functools.partial(k_carry, reverse=reverse), [vm] * 2, [vm] * len(shapes), shapes, "carry"
    )(recv, totals)
    return exchange(back), *near(*gain), totals


def body(queries, key_vectors, value_vectors, out_grad, norm_gain, decay_rates, segment_ids):
    hb, sc = head_block(), scalars()
    big = 9 * 2 * L * L * D * NH
    flat = pltpu.VMEM((L, NH * D), F32)
    q, k, v, rates, segs = far(queries, key_vectors, value_vectors, decay_rates, segment_ids)
    vm, work = near_block(), idle()
    payload = one_call(
        k_state,
        [work] * 4,
        vm,
        sds((G * PR, D)),
        "state",
        big // 6,
        [pltpu.VMEM((L, NH * D), F32)] * 2
        + [SMEM((L,), jnp.int32), SMEM((NH,), F32), pltpu.SemaphoreType.DMA((2 * NH + 2,))],
    )(segs, rates, k, v)
    local_out, bnd, con = heads_call(
        k_local,
        [sc, sc, hb, hb, hb, whole(NH * D)],
        [hb, sc, whole(16, D)],
        [flat, pltpu.HBM((8,), jnp.int32), pltpu.VMEM((16, D), F32)],
        big,
        name="local",
    )(segs, rates, q, k, v, *far(norm_gain))
    (bnd,) = far(bnd)
    (con,) = near(con)
    carry, _ = scan_groups(payload, False)
    out, red = one_call(
        k_norm, [vm] * 5, [vm, vm], [flat, sds((64, D))], "norm", big // 6
    )(con, queries, carry, *near(local_out), out_grad)
    sums = exchange(red, "head", None)
    grad_out, payload = one_call(
        k_grad,
        [vm] * 5,
        [vm, vm],
        [flat, sds((G * PR, D))],
        "grad",
        big // 6,
    )(con, sums, out_grad, *near(out), queries)
    (grad_out,) = near(grad_out)
    back, gain, totals = scan_groups(payload, True)
    dq, both = heads_call(
        k_back,
        [sc, sc, hb, hb, hb, hb, rows_block(D), work],
        [hb, pl.BlockSpec((2, L, D), lambda h: (0, 0, h))],
        [pltpu.HBM((L, NH * D), BF16), pltpu.VMEM((2, L, NH * D), F32)],
        big,
        name="back",
    )(bnd, rates, q, k, v, *far(grad_out), carry, totals)
    dk, dv, gain_grad = one_call(
        k_final,
        [vm] * 6,
        [work, work, vm],
        [pltpu.HBM((L, NH * D), BF16)] * 2 + [sds((NH * D,))],
        "final",
        big // 6,
        [pltpu.VMEM((L, NH * D), BF16)] * 2 + [pltpu.SemaphoreType.DMA((2 * NH,))],
    )(con, key_vectors, value_vectors, back, *near(both), gain)
    return dq, dk, dv, gain_grad


def solution(mesh):
    return jax.shard_map(
        body,
        mesh=mesh,
        in_specs=(
            P("seq", "head"),
            P("seq", "head"),
            P("seq", "head"),
            P("seq", "head"),
            P("head"),
            P("head"),
            P("seq"),
        ),
        out_specs=(P("seq", "head"), P("seq", "head"), P("seq", "head"), P("head")),
        check_vma=False,
    )
```
